32 devices in a mesh: dp: 4 (over y, core), fsdp: 8 (over z, x).
Axes of the slice: x: 2, y: 2, z: 4, core: 2. Of those that a mesh axis runs over, the one named last changes fastest.
Arguments:
- tokens: bfloat16 [64, 512, 768], P(('dp', 'fsdp')), may hold values from -6 to 6
- cotangent: bfloat16 [64, 512, 768], P(('dp', 'fsdp')), may hold values from -6 to 6
- lengths: int32 [4, 16], P('dp'), may hold values from 1 to 512, 6144 in all within a row
- deal: int32 [4, 16], P('dp'), may hold values from 0 to 15, each once within a row
- w_query: bfloat16 [768, 768], P(('dp', 'fsdp')), may hold values from -0.21875 to 0.21875
- b_query: bfloat16 [768], P(('dp', 'fsdp')), may hold values from -1 to 1
- w_key: bfloat16 [768, 768], P(('dp', 'fsdp')), may hold values from -0.21875 to 0.21875
- w_value: bfloat16 [768, 768], P(('dp', 'fsdp')), may hold values from -0.21875 to 0.21875
- b_value: bfloat16 [768], P(('dp', 'fsdp')), may hold values from -1 to 1
- w_out: bfloat16 [768, 768], P(('dp', 'fsdp')), may hold values from -1.25 to 1.25
- b_out: bfloat16 [768], P(('dp', 'fsdp')), may hold values from -1 to 1
- norm1_gain: bfloat16 [768], P(('dp', 'fsdp')), may hold values from 0.5 to 1.5
- norm1_bias: bfloat16 [768], P(('dp', 'fsdp')), may hold values from -1 to 1
- w_in: bfloat16 [768, 3072], P(('dp', 'fsdp')), may hold values from -0.21875 to 0.21875
- b_in: bfloat16 [3072], P(('dp', 'fsdp')), may hold values from -1 to 1
- w_down: bfloat16 [3072, 768], P(('dp', 'fsdp')), may hold values from -0.109375 to 0.109375
- b_down: bfloat16 [768], P(('dp', 'fsdp')), may hold values from -1 to 1
- norm2_gain: bfloat16 [768], P(('dp', 'fsdp')), may hold values from 0.5 to 1.5
- norm2_bias: bfloat16 [768], P(('dp', 'fsdp')), may hold values from -1 to 1
Outputs:
- layer_out: bfloat16 [64, 512, 768], P(('dp', 'fsdp'))
- input_grad: bfloat16 [64, 512, 768], P(('dp', 'fsdp'))
- grad_w_query: float32 [768, 768], P(('dp', 'fsdp'))
- grad_b_query: float32 [768], P(('dp', 'fsdp'))
- grad_w_key: float32 [768, 768], P(('dp', 'fsdp'))
- grad_w_value: float32 [768, 768], P(('dp', 'fsdp'))
- grad_b_value: float32 [768], P(('dp', 'fsdp'))
- grad_w_out: float32 [768, 768], P(('dp', 'fsdp'))
- grad_b_out: float32 [768], P(('dp', 'fsdp'))
- grad_norm1_gain: float32 [768], P(('dp', 'fsdp'))
- grad_norm1_bias: float32 [768], P(('dp', 'fsdp'))
- grad_w_in: float32 [768, 3072], P(('dp', 'fsdp'))
- grad_b_in: float32 [3072], P(('dp', 'fsdp'))
- grad_w_down: float32 [3072, 768], P(('dp', 'fsdp'))
- grad_b_down: float32 [768], P(('dp', 'fsdp'))
- grad_norm2_gain: float32 [768], P(('dp', 'fsdp'))
- grad_norm2_bias: float32 [768], P(('dp', 'fsdp'))
The draws below stay inside these ranges and needn't reach their ends.
Inputs may be any that keep to these rules, and one draw needn't show every extreme that they name: A row holds the lengths of one group's 16 sequences in the given order; it sums to 6144 and its longest is exactly 512. `deal`: each row is a permutation; bucket b of a group is slot b % 2 of the group's device b // 2 along fsdp.
All inputs are finite; a program needn't handle non-finite values.
Results may differ from the reference program's by a relative error of at most 0.014.
Values may be sent and summed in bfloat16 or wider, within the bound.
No kernel may reach another device: no remote copies, remote signals or barrier semaphores. Data moves between devices by JAX's collectives and lax.ppermute only.
A program may use at most 192 MiB of HBM per device.

```python
import math
import jax
import jax.numpy as jnp
import numpy as np
from jax import lax

D = 768
HEADS = 12
HD = 64
FF = 3072
CAP = 512
NSG = 16
SEQS = 64
N_DP = 4


def block_scale(own_key, dims, shards, least, top_value):
    factor_of = 1.0
    for axis_at, blocks in shards:
        draws = jax.random.uniform(jax.random.fold_in(jax.random.fold_in(own_key, 6), axis_at), (blocks,), jnp.float32, least / len(shards), top_value / len(shards))
        factor_of = factor_of * jnp.repeat(jnp.exp(draws), dims[axis_at] // blocks).reshape((-1,) + (1,) * (len(dims) - 1 - axis_at))
    return factor_of


def split_up(amount, total, most, skew):
    weights = [(1 << 20) // math.isqrt(rank ** skew) + 1 for rank in range(2, amount + 1)]
    surplus, given = total - most - (amount - 1), [1] * (amount - 1)
    while surplus > 0:
        free = [i for i in range(amount - 1) if given[i] < most]
        pool, budget = sum([weights[i] for i in free]), surplus
        for i in free:
            extra = min(most - given[i], max(1, budget * weights[i] // pool), surplus)
            given[i] = given[i] + extra
            surplus = surplus - extra
    return np.array([most] + given)


def uneven_parts(rng, amount, total, bound, slope):
    if amount == 2:
        one = jax.random.randint(rng, (), max(1, total - bound), min(bound, total - 1) + 1)
        return jnp.stack([one, total - one])
    tallies = jnp.asarray(split_up(amount, total, bound, slope), jnp.int32)
    twos = (amount - 1) // 2
    donor, sink = tallies[1:1 + 2 * twos:2], tallies[2:2 + 2 * twos:2]
    slack = jnp.minimum(donor - 1, bound - sink)
    moved = jax.random.randint(jax.random.fold_in(rng, 1), (twos,), 0, 1 << 20) % (slack + 1)
    tallies = tallies.at[1:1 + 2 * twos:2].set(donor - moved).at[2:2 + 2 * twos:2].set(sink + moved)
    return tallies[jax.random.permutation(jax.random.fold_in(rng, 2), amount)]


def normal_values(stream_key, dims, scale, bound, cuts=(), kind=jnp.bfloat16):
    array = jax.random.normal(stream_key, dims, jnp.float32) * scale
    if len(cuts) > 0:
        array = block_scale(stream_key, dims, cuts, -0.22, 0.18) * array
    return jnp.clip(array, min=-bound, max=bound).astype(kind)


def setup_inputs(seed: int = 0) -> dict:
    key_of = jax.random.split(jax.random.key(seed), 20)
    tokens = normal_values(key_of[0], (SEQS, CAP, D), 1.0, 6.0, ((0, 32),))
    cotangent = normal_values(key_of[1], (SEQS, CAP, D), 1.0, 6.0, ((0, 32),))
    lengths = jax.vmap(lambda own: uneven_parts(own, NSG, 3 * NSG * CAP // 4, CAP, 2))(jax.random.split(key_of[2], N_DP)).reshape((N_DP, NSG)).astype(jnp.int32)
    deal = jax.vmap(lambda own: jax.random.permutation(own, NSG))(jax.random.split(key_of[3], N_DP)).reshape((N_DP, NSG)).astype(jnp.int32)
    w_query = normal_values(key_of[4], (D, D), D ** -0.5, 0.21875, ((0, 32),))
    b_query = normal_values(key_of[5], (D,), 0.2, 1.0, ((0, 32),))
    w_key = normal_values(key_of[6], (D, D), D ** -0.5, 0.21875, ((0, 32),))
    w_value = normal_values(key_of[7], (D, D), D ** -0.5, 0.21875, ((0, 32),))
    b_value = normal_values(key_of[8], (D,), 0.2, 1.0, ((0, 32),))
    w_out = normal_values(key_of[9], (D, D), (D // 32) ** -0.5, 1.25, ((0, 32),))
    b_out = normal_values(key_of[10], (D,), 0.2, 1.0, ((0, 32),))
    norm1_gain = jnp.clip(1.0 + 0.1 * jax.random.normal(key_of[11], (D,), jnp.float32), 0.5, 1.5).astype(jnp.bfloat16)
    norm1_bias = normal_values(key_of[12], (D,), 0.2, 1.0, ((0, 32),))
    w_in = normal_values(key_of[13], (D, FF), D ** -0.5, 0.21875, ((0, 32),))
    b_in = normal_values(key_of[14], (FF,), 0.2, 1.0, ((0, 32),))
    w_down = normal_values(key_of[15], (FF, D), FF ** -0.5, 0.109375, ((0, 32),))
    b_down = normal_values(key_of[16], (D,), 0.2, 1.0, ((0, 32),))
    norm2_gain = jnp.clip(1.0 + 0.1 * jax.random.normal(key_of[17], (D,), jnp.float32), 0.5, 1.5).astype(jnp.bfloat16)
    norm2_bias = normal_values(key_of[18], (D,), 0.2, 1.0, ((0, 32),))
    return dict(tokens=tokens, cotangent=cotangent, lengths=lengths, deal=deal, w_query=w_query, b_query=b_query, w_key=w_key, w_value=w_value, b_value=b_value, w_out=w_out, b_out=b_out, norm1_gain=norm1_gain, norm1_bias=norm1_bias, w_in=w_in, b_in=b_in, w_down=w_down, b_down=b_down, norm2_gain=norm2_gain, norm2_bias=norm2_bias)


norm_eps = 1e-12
half_root = 0.7071067811865476

@jax.custom_vjp
def low(v):
    return lax.optimization_barrier(v.astype(jnp.bfloat16)).astype(jnp.float32)

@jax.custom_vjp
def low_back(v):
    return v

def low_keep(v):
    return (low(v), None)

def low_pass(kept, grad):
    return (grad,)

def back_keep(v):
    return (v, None)

def back_low(kept, grad):
    return (low(grad),)
low.defvjp(low_keep, low_pass)
low_back.defvjp(back_keep, back_low)

def normalize(values, gain, shift):
    centre = values - lax.optimization_barrier(jnp.mean(values, axis=-1, keepdims=True))
    spread = lax.rsqrt(lax.optimization_barrier(jnp.mean(centre * centre, axis=-1, keepdims=True)) + norm_eps)
    return centre * spread * gain + shift

def gelu_value(values):
    return 0.5 * values * (1.0 + lax.erf(values * half_root))

def layer_sequence(params, inputs, length):
    w_query, b_query, w_key, w_value, b_value, w_out, b_out, norm1_gain, norm1_bias, w_in, b_in, w_down, b_down, norm2_gain, norm2_bias = params
    highest = lax.Precision.HIGHEST
    rows = inputs.shape[0]
    valid = jnp.arange(rows) < length
    query = low(low_back(jnp.dot(inputs, w_query, precision=highest) + b_query))
    keys = low(low_back(jnp.dot(inputs, w_key, precision=highest)))
    values = low(low_back(jnp.dot(inputs, w_value, precision=highest) + b_value))
    query_heads = query.reshape(rows, HEADS, HD)
    key_heads = keys.reshape(rows, HEADS, HD)
    value_heads = values.reshape(rows, HEADS, HD)
    raw = jnp.einsum('qhd,khd->hqk', query_heads, key_heads, precision=highest)
    scores = low_back(raw * HD ** (-0.5))
    scores = jnp.where(valid[None, None, :], scores, -1e+30)
    top = lax.optimization_barrier(jnp.max(scores, axis=-1, keepdims=True))
    total = jnp.log(lax.optimization_barrier(jnp.sum(jnp.exp(scores - top), axis=-1, keepdims=True))) + top
    probs = low(jnp.exp(scores - total))
    context = jnp.einsum('hqk,khd->qhd', probs, value_heads, precision=highest).reshape(rows, -1)
    context = low(low_back(context))
    attended = low_back(jnp.dot(context, w_out, precision=highest) + b_out)
    middle = normalize(inputs + attended, norm1_gain, norm1_bias)
    hidden = low_back(jnp.dot(low(middle), w_in, precision=highest) + b_in)
    active = low(gelu_value(hidden))
    branch = low_back(jnp.dot(active, w_down, precision=highest) + b_down)
    result = normalize(middle + branch, norm2_gain, norm2_bias)
    return jnp.where(valid[:, None], result, 0.0)

def reference(tokens, cotangent, lengths, deal, w_query, b_query, w_key, w_value, b_value, w_out, b_out, norm1_gain, norm1_bias, w_in, b_in, w_down, b_down, norm2_gain, norm2_bias):
    params = tuple((weight.astype(jnp.float32) for weight in (w_query, b_query, w_key, w_value, b_value, w_out, b_out, norm1_gain, norm1_bias, w_in, b_in, w_down, b_down, norm2_gain, norm2_bias)))
    group_base = (jnp.arange(lengths.shape[0], dtype=jnp.int32) * lengths.shape[1])[:, None]
    placed = (deal.astype(jnp.int32) + group_base).reshape(-1).astype(jnp.int32)
    seq_lengths = lengths.reshape(-1).astype(jnp.int32)
    inputs = tokens.astype(jnp.float32)
    upstream = jnp.take(cotangent.astype(jnp.float32), placed, axis=0)
    stepper = jax.checkpoint(layer_sequence)

    def forward_all(weights, source):

        def visit(carry, pair):
            return (carry, stepper(weights, pair[0], pair[1]))
        final, outputs = lax.scan(visit, jnp.zeros((), jnp.float32), (source, seq_lengths))
        return outputs
    outputs, pull = jax.vjp(forward_all, params, inputs)
    grad_params, grad_inputs = pull(upstream)
    layer_out = jnp.zeros_like(outputs).at[placed].set(outputs).astype(jnp.bfloat16)
    return (layer_out, grad_inputs.astype(jnp.bfloat16), grad_params[0], grad_params[1], grad_params[2], grad_params[3], grad_params[4], grad_params[5], grad_params[6], grad_params[7], grad_params[8], grad_params[9], grad_params[10], grad_params[11], grad_params[12], grad_params[13], grad_params[14])
```

```python
import jax
import jax.numpy as jnp
from jax import lax
from jax.sharding import PartitionSpec as P

HD = 64
LINE = 4
BOTH = ("dp", "fsdp")
bf16 = jnp.bfloat16
f32 = jnp.float32

norm_eps = 1e-12
half_root = 0.7071067811865476
slope_scale = 0.3989422804014327


class Grid:
    def __init__(self, mesh):
        self.dp = mesh.shape["dp"]
        self.fsdp = mesh.shape["fsdp"]
        self.total = self.dp * self.fsdp
        nx = self.fsdp // LINE
        ny = self.dp // 2
        self.size = {"y": ny, "core": 2, "z": LINE, "x": nx}
        self.stride = {"x": 1, "z": nx, "core": self.fsdp, "y": 2 * self.fsdp}

    def place(self, axis):
        me = lax.axis_index("dp") * self.fsdp + lax.axis_index("fsdp")
        return (me // self.stride[axis]) % self.size[axis]

    def swap(self, array, axis, step):
        mask = self.stride[axis] * step
        return lax.ppermute(array, BOTH, [(i, i ^ mask) for i in range(self.total)])


AXES = ("y", "core", "z", "x")


def gather(grid, shard, order):
    held = shard
    have = []
    for axis in order:
        size = grid.size[axis]
        me = grid.place(axis)
        parts = [held] + [grid.swap(held, axis, step) for step in range(1, size)]
        bit = 1
        while bit < size:
            flip = (me & bit) != 0
            parts = [jnp.where(flip, parts[j ^ bit], parts[j]) for j in range(size)]
            bit *= 2
        at = sum(AXES.index(other) < AXES.index(axis) for other in have)
        held = jnp.stack(parts, axis=at)
        have.append(axis)
    return held.reshape((-1,) + shard.shape[1:])


def scatter_sum(grid, terms, order):
    rows = terms.shape[0] // grid.total
    held = terms.reshape(tuple(grid.size[axis] for axis in AXES) + (rows,) + terms.shape[1:])
    have = list(AXES)
    for axis in order:
        size = grid.size[axis]
        me = grid.place(axis)
        at = have.index(axis)
        kept = lax.dynamic_index_in_dim(held, me, at, keepdims=False)
        got = [
            grid.swap(
                lax.dynamic_index_in_dim(held, me ^ step, at, keepdims=False).astype(bf16),
                axis,
                step,
            )
            for step in range(1, size)
        ]
        held = kept
        for one in got:
            held = held + one.astype(f32)
        have.remove(axis)
    return held


def standardize(values):
    centre = values - jnp.mean(values, axis=-1, keepdims=True)
    spread = lax.rsqrt(jnp.mean(centre * centre, axis=-1, keepdims=True) + norm_eps)
    return (centre * spread, spread)


def norm_back(d_normed, normed, spread):
    return spread * (
        d_normed
        - jnp.mean(d_normed, axis=-1, keepdims=True)
        - normed * jnp.mean(d_normed * normed, axis=-1, keepdims=True)
    )


def gelu_value(values):
    return 0.5 * values * (1.0 + lax.erf(values * half_root))


def gelu_slope(values):
    return (
        0.5 * (1.0 + lax.erf(values * half_root))
        + values * jnp.exp(-0.5 * values * values) * slope_scale
    )


def matmul(left, right):
    return jnp.dot(left, right, preferred_element_type=f32)


def left_times(left, right):
    return jnp.einsum("ti,to->io", left, right, preferred_element_type=f32)


def right_times(grads, weight):
    return jnp.einsum("to,io->ti", grads, weight, preferred_element_type=f32)


def pieces_out(array, count):
    slots, rows, width = array.shape
    return array.reshape(slots, count, rows // count, width).transpose(1, 0, 2, 3)


def reorder(array, source):
    count = lax.axis_size("fsdp")
    slots, rows, width = array.shape
    spread = lax.all_to_all(pieces_out(array, count), "fsdp", 0, 0, tiled=True)
    spread = spread.reshape(count * slots, rows // count, width)
    spread = jnp.take(spread, source, axis=0, mode="clip").reshape(count, slots, rows // count, width)
    joined = lax.all_to_all(spread, "fsdp", 0, 0, tiled=True)
    return joined.transpose(1, 0, 2, 3).reshape(slots, rows, width)


def per_device(grid, *args):
    (
        tokens,
        cotangent,
        lengths,
        deal,
        w_query,
        b_query,
        w_key,
        w_value,
        b_value,
        w_out,
        b_out,
        gain_one,
        shift_one,
        w_in,
        b_in,
        w_down,
        b_down,
        gain_two,
        shift_two,
    ) = args
    slots, rows, width = tokens.shape
    hidden_width = w_in.shape[1]
    position = lax.axis_index("fsdp")
    deal_row = deal[0]
    my_lengths = lax.dynamic_slice_in_dim(lengths[0], position * slots, slots)
    spots = jnp.arange(deal_row.shape[0], dtype=jnp.int32)
    inverse = jnp.sum(
        jnp.where(deal_row[None, :] == spots[:, None], spots[None, :], 0), axis=1
    )

    own = jnp.concatenate([w_query, w_key, w_value], axis=1)
    third = own.shape[1] // 3
    qkv = jnp.concatenate(
        [
            gather(grid, own[:, :third], ("z", "x", "y", "core")),
            gather(grid, own[:, third : 2 * third], ("x", "y", "z", "core")),
            gather(grid, own[:, 2 * third :], ("y", "z", "x", "core")),
        ],
        axis=1,
    )
    singles = (b_query, b_value, b_out, gain_one, shift_one, b_in, b_down, gain_two, shift_two)
    small = jnp.concatenate(singles)
    small = lax.all_to_all(
        jnp.broadcast_to(small[None, :], (grid.total, small.shape[0])), BOTH, 0, 0, tiled=True
    )
    vectors = []
    at = 0
    for one in singles:
        vectors.append(small[:, at : at + one.shape[0]].reshape(-1).astype(f32))
        at += one.shape[0]
    bq, bv, bo, g1, s1, bi, bd, g2, s2 = vectors

    wo = gather(grid, w_out, ("z", "x", "y", "core"))
    wi = gather(grid, w_in, ("z", "x", "y", "core"))
    wd = gather(grid, w_down, ("z", "x", "y", "core"))

    upstream = reorder(cotangent, deal_row)

    total_rows = slots * rows
    inputs = tokens.reshape(total_rows, width)
    valid = jnp.arange(rows)[None, :] < my_lengths[:, None]
    valid_row = valid.reshape(total_rows)[:, None]

    no_bias = jnp.zeros_like(bq)
    fused = (matmul(inputs, qkv) + jnp.concatenate([bq, no_bias, bv])).astype(bf16)
    query, key_rows, value_rows = (
        fused[:, i * width : (i + 1) * width].reshape(slots, rows, -1, HD) for i in range(3)
    )

    def scores_of():
        raw = jnp.einsum("sqhd,skhd->shqk", query, key_rows, preferred_element_type=f32)
        return jnp.where(valid[:, None, None, :], raw * HD ** (-0.5), -1e30)

    scores = scores_of()
    top = jnp.max(scores, axis=-1, keepdims=True)
    total = jnp.log(jnp.sum(jnp.exp(scores - top), axis=-1, keepdims=True)) + top
    probs = jnp.exp(scores - total).astype(bf16)
    context = (
        jnp.einsum("shqk,skhd->sqhd", probs, value_rows, preferred_element_type=f32)
        .reshape(total_rows, width)
        .astype(bf16)
    )
    middle_norm, middle_spread = standardize(inputs.astype(f32) + matmul(context, wo) + bo)
    middle = middle_norm * g1 + s1
    middle_low = middle.astype(bf16)
    hidden = matmul(middle_low, wi) + bi
    active = gelu_value(hidden).astype(bf16)
    final_norm, final_spread = standardize(middle + matmul(active, wd) + bd)
    output = jnp.where(valid_row, final_norm * g2 + s2, 0.0).astype(bf16)
    layer_out = reorder(output.reshape(slots, rows, width), inverse)

    d_result = jnp.where(valid_row, upstream.reshape(total_rows, width).astype(f32), 0.0)
    grad_g2 = jnp.sum(d_result * final_norm, axis=0)
    grad_s2 = jnp.sum(d_result, axis=0)
    d_final = norm_back(d_result * g2, final_norm, final_spread)
    d_branch = d_final.astype(bf16)
    grad_bd = jnp.sum(d_branch.astype(f32), axis=0)
    shard_wd = scatter_sum(grid, left_times(active, d_branch), ("core", "y", "x", "z"))
    d_hidden = (right_times(d_branch, wd) * gelu_slope(hidden)).astype(bf16)
    grad_bi = jnp.sum(d_hidden.astype(f32), axis=0)
    shard_wi = scatter_sum(grid, left_times(middle_low, d_hidden), ("core", "y", "x", "z"))
    d_middle = d_final + right_times(d_hidden, wi)
    grad_g1 = jnp.sum(d_middle * middle_norm, axis=0)
    grad_s1 = jnp.sum(d_middle, axis=0)
    d_sum = norm_back(d_middle * g1, middle_norm, middle_spread)
    d_attended = d_sum.astype(bf16)
    grad_bo = jnp.sum(d_attended.astype(f32), axis=0)
    shard_wo = scatter_sum(grid, left_times(context, d_attended), ("core", "y", "x", "z"))
    d_context = right_times(d_attended, wo).astype(bf16).reshape(slots, rows, -1, HD)
    probs = jnp.exp(scores_of() - total)
    d_probs = jnp.einsum("sqhd,skhd->shqk", d_context, value_rows, preferred_element_type=f32)
    d_value = jnp.einsum(
        "shqk,sqhd->skhd", probs.astype(bf16), d_context, preferred_element_type=f32
    )
    d_scores = (probs * (d_probs - jnp.sum(probs * d_probs, axis=-1, keepdims=True))).astype(bf16)
    scale = HD ** (-0.5)
    d_query = (
        jnp.einsum("shqk,skhd->sqhd", d_scores, key_rows, preferred_element_type=f32) * scale
    )
    d_key = jnp.einsum("shqk,sqhd->skhd", d_scores, query, preferred_element_type=f32) * scale
    d_fused = jnp.concatenate(
        [one.reshape(total_rows, width).astype(bf16) for one in (d_query, d_key, d_value)], axis=1
    )
    grad_fused = jnp.sum(d_fused.astype(f32), axis=0)
    shard_qkv = scatter_sum(grid, left_times(inputs, d_fused), ("core", "y", "x", "z"))
    input_grad = (d_sum + right_times(d_fused, qkv)).astype(bf16).reshape(slots, rows, width)

    grads = (
        grad_fused[:width],
        grad_fused[2 * width :],
        grad_bo,
        grad_g1,
        grad_s1,
        grad_bi,
        grad_bd,
        grad_g2,
        grad_s2,
    )
    small = jnp.concatenate([one.reshape(grid.total, -1) for one in grads], axis=1)
    small = jnp.sum(lax.all_to_all(small, BOTH, 0, 0, tiled=True), axis=0)
    parts = []
    at = 0
    for one in singles:
        parts.append(small[at : at + one.shape[0]])
        at += one.shape[0]
    pbq, pbv, pbo, pg1, ps1, pbi, pbd, pg2, ps2 = parts
    return (
        layer_out,
        input_grad,
        shard_qkv[:, :width],
        pbq,
        shard_qkv[:, width : 2 * width],
        shard_qkv[:, 2 * width :],
        pbv,
        shard_wo,
        pbo,
        pg1,
        ps1,
        shard_wi,
        pbi,
        shard_wd,
        pbd,
        pg2,
        ps2,
    )


def solution(mesh):
    grid = Grid(mesh)
    rows3 = P(BOTH, None, None)
    rows2 = P(BOTH, None)
    rows1 = P(BOTH)
    table = P("dp", None)
    kinds = (2, 1, 2, 2, 1, 2, 1, 1, 1, 2, 1, 2, 1, 1, 1)
    placed = tuple(rows2 if kind == 2 else rows1 for kind in kinds)

    def step(*args):
        return per_device(grid, *args)

    return jax.shard_map(
        step,
        mesh=mesh,
        in_specs=(rows3, rows3, table, table) + placed,
        out_specs=(rows3, rows3) + placed,
        check_vma=False,
    )
```

```python
import itertools

import jax
import jax.numpy as jnp
from jax import lax
from jax.experimental import pallas as pl
from jax.experimental.pallas import tpu as pltpu
from jax.sharding import PartitionSpec as P

HD = 64
WIDE = 2 * HD
NEG = -1e30
LINE = 4
BOTH = ("dp", "fsdp")
bf16 = jnp.bfloat16
f32 = jnp.float32

norm_eps = 1e-12
half_root = 0.7071067811865476
slope_scale = 0.3989422804014327


class Grid:
    def __init__(self, mesh):
        self.dp = mesh.shape["dp"]
        self.fsdp = mesh.shape["fsdp"]
        self.total = self.dp * self.fsdp
        nx = self.fsdp // LINE
        ny = self.dp // 2
        self.size = {"y": ny, "core": 2, "zh": 2, "zl": 2, "x": nx}
        self.stride = {"x": 1, "zl": nx, "zh": 2 * nx, "core": self.fsdp, "y": 2 * self.fsdp}

    def place(self, axis):
        me = lax.axis_index("dp") * self.fsdp + lax.axis_index("fsdp")
        return (me // self.stride[axis]) % self.size[axis]

    def spot(self):
        line = self.place("zh") * 2 + self.place("zl")
        return jnp.stack([self.place("y"), self.place("core"), line, self.place("x")]).astype(
            jnp.int32
        )

    def swap(self, array, axis, step):
        mask = self.stride[axis] * step
        return lax.ppermute(array, BOTH, [(i, i ^ mask) for i in range(self.total)])


AXES = ("y", "core", "zh", "zl", "x")


def place_kernel(spot, *refs, keys):
    out = refs[-1]
    for part, (y, core, x) in zip(refs, keys):
        out[spot[0] ^ y, spot[1] ^ core, 0, spot[3] ^ x] = part[0]


class Gather:
    def __init__(self, grid, shard):
        self.grid = grid
        self.held = shard

    def fetch(self, array, **steps):
        grid = self.grid
        mask = sum(grid.stride[axis] * step for axis, step in steps.items())
        return lax.ppermute(array, BOTH, [(k, k ^ mask) for k in range(grid.total)])

    def send_line(self):
        return [self.fetch(self.held, zl=step & 1, zh=step >> 1) for step in range(1, LINE)]

    def take_line(self, got):
        parts = [self.held] + list(got)
        me = self.grid.place("zh") * 2 + self.grid.place("zl")
        shape = (LINE,) + self.held.shape
        line = lax.broadcasted_iota(jnp.int32, shape, 0)
        held = parts[-1][None]
        for step in range(LINE - 2, -1, -1):
            held = jnp.where(line == (me ^ step), parts[step][None], held)
        self.held = held

    def send_plane(self):
        sizes = self.grid.size
        self.keys = [(y, x) for y in range(sizes["y"]) for x in range(sizes["x"])]
        return [self.fetch(self.held, y=y, x=x) for y, x in self.keys[1:]]

    def take_plane(self, got):
        self.parts = [self.held] + list(got)

    def send_core(self):
        return [self.fetch(part, core=1) for part in self.parts]

    def whole(self, got):
        grid = self.grid
        rows, wide = self.held.shape[1:]
        keys = [(y, core, x) for core in range(2) for y, x in self.keys]
        shape = (grid.size["y"], 2, LINE, grid.size["x"], rows, wide)
        out = pl.pallas_call(
            lambda *refs: place_kernel(*refs, keys=keys),
            grid_spec=pltpu.PrefetchScalarGridSpec(
                num_scalar_prefetch=1,
                grid=(LINE,),
                in_specs=[pl.BlockSpec((1, rows, wide), lambda i, _: (i, 0, 0))] * len(keys),
                out_specs=pl.BlockSpec(
                    shape[:2] + (1,) + shape[3:], lambda i, _: (0, 0, i, 0, 0, 0)
                ),
            ),
            out_shape=jax.ShapeDtypeStruct(shape, bf16),
            cost_estimate=pl.CostEstimate(
                flops=0, bytes_accessed=4 * grid.total * rows * wide, transcendentals=0
            ),
            name="place",
        )(grid.spot(), *self.parts, *got)
        return out.reshape(grid.total * rows, wide)


def join_kernel(query_ref, key_ref, value_ref, out_ref, in_ref, first_ref, up_ref):
    width = out_ref.shape[1]
    for pair in range(width // WIDE):
        for i, ref in enumerate((query_ref, key_ref, value_ref)):
            at = (pair * 3 + i) * WIDE
            first_ref[:, at : at + WIDE] = ref[:, pair * WIDE : (pair + 1) * WIDE]
    up_ref[:, :width] = out_ref[...]
    up_ref[:, width:] = in_ref[...]


def join(w_query, w_key, w_value, w_out, w_in):
    rows, width = w_query.shape
    return pl.pallas_call(
        join_kernel,
        out_shape=[
            jax.ShapeDtypeStruct((rows, 3 * width), bf16),
            jax.ShapeDtypeStruct((rows, width + w_in.shape[1]), bf16),
        ],
        name="join",
    )(w_query, w_key, w_value, w_out, w_in)


def grad_tall_kernel(spot, left_ref, right_ref, out_ref):
    out_ref[0] = tn(left_ref[...], right_ref[...]).astype(bf16)


def grad_tall(grid, left, right, other):
    rows, tall = left.shape
    wide = right.shape[1]
    ny = grid.size["y"]
    block = tall // (2 * ny)
    return pl.pallas_call(
        grad_tall_kernel,
        grid_spec=pltpu.PrefetchScalarGridSpec(
            num_scalar_prefetch=1,
            grid=(ny,),
            in_specs=[
                pl.BlockSpec((rows, block), lambda y, spot: (0, y * 2 + (spot[1] ^ other))),
                pl.BlockSpec((rows, wide), lambda y, _: (0, 0)),
            ],
            out_specs=pl.BlockSpec((1, block, wide), lambda y, _: (y, 0, 0)),
        ),
        out_shape=jax.ShapeDtypeStruct((ny, block, wide), bf16),
        cost_estimate=pl.CostEstimate(
            flops=rows * tall * wide * 2, bytes_accessed=rows * tall * 2, transcendentals=0
        ),
        name="grad_tall",
    )(grid.spot(), left, right)


STRIP = 384


def grad_wide_kernel(spot, left_ref, right_ref, *refs):
    own_ref, other_ref, turned, total = refs[-4:]

    @pl.when(pl.program_id(0) == 0)
    def _():
        turned[...] = left_ref[...].T

    total[...] = jnp.dot(turned[...], right_ref[...], preferred_element_type=f32)
    ny, block = own_ref.shape[:2]
    core = spot[1]
    for y in range(ny):
        at = pl.multiple_of((2 * y + core) * block, 16)
        own_ref[y] = total[pl.ds(at, block), :].astype(bf16)
        at = pl.multiple_of((2 * y + 1 - core) * block, 16)
        other_ref[y] = total[pl.ds(at, block), :].astype(bf16)


def grad_wide(grid, left, right, wide=None, first=0, base=None):
    rows, tall = left.shape
    wide = wide or right.shape[1]
    ny = grid.size["y"]
    block = tall // (2 * ny)
    at = first // STRIP
    made = pl.BlockSpec((ny, block, STRIP), lambda j, _: (0, 0, j + at))
    given = () if base is None else tuple(base)
    return pl.pallas_call(
        grad_wide_kernel,
        grid_spec=pltpu.PrefetchScalarGridSpec(
            num_scalar_prefetch=1,
            grid=(right.shape[1] // STRIP,),
            in_specs=[
                pl.BlockSpec((rows, tall), lambda j, _: (0, 0)),
                pl.BlockSpec((rows, STRIP), lambda j, _: (0, j)),
            ]
            + [pl.BlockSpec(memory_space=pl.ANY)] * len(given),
            out_specs=[made, made],
            scratch_shapes=[pltpu.VMEM((tall, rows), bf16), pltpu.VMEM((tall, STRIP), f32)],
        ),
        out_shape=[jax.ShapeDtypeStruct((ny, block, wide), bf16)] * 2,
        input_output_aliases={3: 0, 4: 1} if given else {},
        cost_estimate=pl.CostEstimate(
            flops=rows * tall * right.shape[1] * 2,
            bytes_accessed=2 * rows * (tall + right.shape[1]),
            transcendentals=0,
        ),
        name="grad_wide",
    )(grid.spot(), left, right, *given)


def fold_plane_kernel(spot, own_ref, got_ref, *outs, keys):
    for out, (y, x) in zip(outs, keys):
        at = (spot[0] ^ y, 0, spot[3] ^ x)
        out[0] = (own_ref[at].astype(f32) + got_ref[at].astype(f32)).astype(bf16)


def fold_line_kernel(spot, *refs):
    parts, outs = refs[:-LINE], refs[-LINE:]
    for step, out in enumerate(outs):
        total = parts[0][spot[2] ^ step].astype(f32)
        for part in parts[1:]:
            total = total + part[spot[2] ^ step].astype(f32)
        out[...] = total.astype(bf16)


class Scatter:
    def __init__(self, grid):
        self.grid = grid

    def fetch(self, array, **steps):
        grid = self.grid
        mask = sum(grid.stride[axis] * step for axis, step in steps.items())
        return lax.ppermute(array, BOTH, [(k, k ^ mask) for k in range(grid.total)])

    def send_core(self, other):
        return self.fetch(other, core=1)

    def send_plane(self, own, got):
        grid = self.grid
        ny, block, wide = own.shape
        nx = grid.size["x"]
        rows = block // (LINE * nx)
        shape = (ny, LINE, nx, rows, wide)
        keys = [(y, x) for y in range(ny) for x in range(nx)]
        whole = pl.BlockSpec((ny, 1, nx, rows, wide), lambda i, _: (0, i, 0, 0, 0))
        parts = pl.pallas_call(
            lambda *refs: fold_plane_kernel(*refs, keys=keys),
            grid_spec=pltpu.PrefetchScalarGridSpec(
                num_scalar_prefetch=1,
                grid=(LINE,),
                in_specs=[whole, whole],
                out_specs=[pl.BlockSpec((1, rows, wide), lambda i, _: (i, 0, 0))] * len(keys),
            ),
            out_shape=[jax.ShapeDtypeStruct((LINE, rows, wide), bf16)] * len(keys),
            cost_estimate=pl.CostEstimate(
                flops=0, bytes_accessed=6 * ny * block * wide, transcendentals=0
            ),
            name="fold_plane",
        )(grid.spot(), own.reshape(shape), got.reshape(shape))
        self.own = parts[0]
        return [self.fetch(part, y=y, x=x) for part, (y, x) in zip(parts[1:], keys[1:])]

    def send_line(self, got):
        rows, wide = self.own.shape[1:]
        parts = pl.pallas_call(
            fold_line_kernel,
            grid_spec=pltpu.PrefetchScalarGridSpec(
                num_scalar_prefetch=1,
                grid=(1,),
                in_specs=[pl.BlockSpec((LINE, rows, wide), lambda i, _: (0, 0, 0))]
                * (1 + len(got)),
                out_specs=[pl.BlockSpec((rows, wide), lambda i, _: (0, 0))] * LINE,
            ),
            out_shape=[jax.ShapeDtypeStruct((rows, wide), bf16)] * LINE,
            cost_estimate=pl.CostEstimate(
                flops=0, bytes_accessed=8 * LINE * rows * wide, transcendentals=0
            ),
            name="fold_line",
        )(self.grid.spot(), self.own, *got)
        self.own = parts[0]
        return [
            self.fetch(part, zl=step & 1, zh=step >> 1)
            for step, part in zip(range(1, LINE), parts[1:])
        ]

    def finish(self, got):
        total = self.own.astype(f32)
        for one in got:
            total = total + one.astype(f32)
        return total


def tie(values, after):
    return lax.optimization_barrier((values, after))


def standardize(values):
    centre = values - jnp.mean(values, axis=-1, keepdims=True)
    spread = lax.rsqrt(jnp.mean(centre * centre, axis=-1, keepdims=True) + norm_eps)
    return (centre * spread, spread)


def norm_back(d_normed, normed, spread):
    return spread * (
        d_normed
        - jnp.mean(d_normed, axis=-1, keepdims=True)
        - normed * jnp.mean(d_normed * normed, axis=-1, keepdims=True)
    )


def gelu_value(values):
    return 0.5 * values * (1.0 + lax.erf(values * half_root))


def gelu_slope(values):
    return (
        0.5 * (1.0 + lax.erf(values * half_root))
        + values * jnp.exp(-0.5 * values * values) * slope_scale
    )


def matmul(left, right):
    return jnp.dot(left, right, preferred_element_type=f32)


def left_times(left, right):
    return jnp.einsum("ti,to->io", left, right, preferred_element_type=f32)


def right_times(grads, weight):
    return jnp.einsum("to,io->ti", grads, weight, preferred_element_type=f32)


def nt(left, right):
    return lax.dot_general(left, right, (((1,), (1,)), ((), ())), preferred_element_type=f32)


def tn(left, right):
    return lax.dot_general(left, right, (((0,), (0,)), ((), ())), preferred_element_type=f32)


def head_lanes(shape, head):
    lane = lax.broadcasted_iota(jnp.int32, shape, 1)
    return (lane >= head * HD) & (lane < (head + 1) * HD)


def score_operands(query, key_rows, length, head):
    rows, wide = query.shape
    lane = lax.broadcasted_iota(jnp.int32, (rows, wide), 1)
    row = lax.broadcasted_iota(jnp.int32, (rows, wide), 0)
    spare = (1 - head) * HD
    mine = head_lanes((rows, wide), head)
    one = jnp.where(lane == spare, 1.0, 0.0).astype(bf16)
    mask = jnp.where(row < length, 0.0, NEG).astype(bf16)
    left = jnp.where(mine, query * bf16(HD ** (-0.5)), one)
    right = jnp.where(lane == spare, mask, key_rows)
    return left, right


def attend_kernel(lengths, fused_ref, context_ref, total_ref, *, first):
    length = lengths[first + pl.program_id(0)]
    query, key_rows, value = (fused_ref[:, i * WIDE : (i + 1) * WIDE] for i in range(3))
    weights, values, scales = [], [], []
    for head in range(2):
        left, right = score_operands(query, key_rows, length, head)
        scores = nt(right, left)
        top = jnp.max(scores, axis=0, keepdims=True)
        raised = jnp.exp(scores - top)
        amount = jnp.sum(raised, axis=0, keepdims=True)
        total_ref[0, 0, head : head + 1, :] = top + jnp.log(amount)
        scales.append(1.0 / amount)
        weights.append(raised.astype(bf16))
        values.append(jnp.where(head_lanes(value.shape, head), value, bf16(0)))
    context = tn(jnp.concatenate(values, axis=0), jnp.concatenate(weights, axis=0))
    context = jnp.concatenate([context[:HD] * scales[0], context[HD:] * scales[1]], axis=0)
    context_ref[...] = context.T.astype(bf16)


def attend(fused, lengths, slots, first, count):
    width = fused.shape[1] // 3
    rows = fused.shape[0] // slots
    pairs = width // WIDE
    return pl.pallas_call(
        lambda *refs: attend_kernel(*refs, first=first),
        grid_spec=pltpu.PrefetchScalarGridSpec(
            num_scalar_prefetch=1,
            grid=(count, pairs),
            in_specs=[pl.BlockSpec((rows, 3 * WIDE), lambda s, h, _: (s + first, h))],
            out_specs=[
                pl.BlockSpec((rows, WIDE), lambda s, h, _: (s, h)),
                pl.BlockSpec((1, 1, 2, rows), lambda s, h, _: (s, h, 0, 0)),
            ],
        ),
        out_shape=[
            jax.ShapeDtypeStruct((count * rows, width), bf16),
            jax.ShapeDtypeStruct((count, pairs, 2, rows), f32),
        ],
        cost_estimate=pl.CostEstimate(
            flops=4 * count * rows * rows * width * 4,
            bytes_accessed=8 * count * rows * width,
            transcendentals=count * pairs * 2 * rows * rows,
        ),
        name="attend",
    )(lengths, fused)


def attend_back_kernel(lengths, fused_ref, total_ref, up_ref, d_ref, sums_ref):
    length = lengths[pl.program_id(1)]
    query, key_rows, value = (fused_ref[:, i * WIDE : (i + 1) * WIDE] for i in range(3))
    up = up_ref[...]
    weights, slopes, ups, queries, keys = [], [], [], [], []
    for head in range(2):
        left, right = score_operands(query, key_rows, length, head)
        mine = head_lanes(query.shape, head)
        scores = nt(right, left)
        probs = jnp.exp(scores - total_ref[0, 0, head : head + 1, :])
        masked = jnp.where(mine, up, bf16(0))
        d_probs = nt(value, masked)
        product = probs * d_probs
        d_scores = product - probs * jnp.sum(product, axis=0, keepdims=True)
        weights.append(probs.astype(bf16))
        slopes.append(d_scores.astype(bf16))
        ups.append(masked)
        queries.append(jnp.where(mine, query * bf16(HD ** (-0.5)), bf16(0)))
        keys.append(jnp.where(mine, key_rows * bf16(HD ** (-0.5)), bf16(0)))
    d_value = jnp.dot(
        jnp.concatenate(weights, axis=1), jnp.concatenate(ups, axis=0), preferred_element_type=f32
    ).astype(bf16)
    d_key = jnp.dot(
        jnp.concatenate(slopes, axis=1), jnp.concatenate(queries, axis=0), preferred_element_type=f32
    ).astype(bf16)
    d_query = tn(jnp.concatenate(keys, axis=0), jnp.concatenate(slopes, axis=0)).T.astype(bf16)
    d_ref[:, 0:WIDE] = d_query
    d_ref[:, WIDE : 2 * WIDE] = d_key
    d_ref[:, 2 * WIDE :] = d_value
    sums_ref[0, 0:1, :] = jnp.sum(d_query.astype(f32), axis=0, keepdims=True)
    sums_ref[0, 1:2, :] = jnp.sum(d_value.astype(f32), axis=0, keepdims=True)


def attend_back(fused, totals, up, lengths, slots, first, count):
    width = fused.shape[1] // 3
    rows = fused.shape[0] // slots
    return pl.pallas_call(
        attend_back_kernel,
        grid_spec=pltpu.PrefetchScalarGridSpec(
            num_scalar_prefetch=1,
            grid=(count, slots),
            in_specs=[
                pl.BlockSpec((rows, 3 * WIDE), lambda h, s, _: (s, first + h)),
                pl.BlockSpec((1, 1, 2, rows), lambda h, s, _: (s, first + h, 0, 0)),
                pl.BlockSpec((rows, WIDE), lambda h, s, _: (s, first + h)),
            ],
            out_specs=[
                pl.BlockSpec((rows, 3 * WIDE), lambda h, s, _: (s, h)),
                pl.BlockSpec((1, 2, WIDE), lambda h, s, _: (s, 0, h)),
            ],
        ),
        out_shape=[
            jax.ShapeDtypeStruct((slots * rows, count * 3 * WIDE), bf16),
            jax.ShapeDtypeStruct((slots, 2, count * WIDE), f32),
        ],
        cost_estimate=pl.CostEstimate(
            flops=10 * slots * rows * rows * count * WIDE * 4,
            bytes_accessed=16 * slots * rows * count * WIDE,
            transcendentals=slots * count * 2 * rows * rows,
        ),
        name="attend_back",
    )(lengths, fused, totals, up)


def interleave(query, key_rows, value):
    lead = query.shape[0]
    return jnp.stack([one.reshape(lead, -1, WIDE) for one in (query, key_rows, value)], axis=2).reshape(
        lead, -1
    )


def pieces_out(array, count):
    slots, rows, width = array.shape
    return array.reshape(slots, count, rows // count, width).transpose(1, 0, 2, 3)


def spread_out(array):
    count = lax.axis_size("fsdp")
    return lax.all_to_all(pieces_out(array, count), "fsdp", 0, 0, tiled=True)


def bring_in(spread, source):
    count, slots, short, width = spread.shape
    spread = spread.reshape(count * slots, short, width)
    spread = jnp.take(spread, source, axis=0, mode="clip").reshape(count, slots, short, width)
    return lax.all_to_all(spread, "fsdp", 0, 0, tiled=True)


def joined(pieces):
    count, slots, short, width = pieces.shape
    return pieces.transpose(1, 0, 2, 3).reshape(slots, count * short, width)


def per_device(grid, *args):
    (
        tokens,
        cotangent,
        lengths,
        deal,
        w_query,
        b_query,
        w_key,
        w_value,
        b_value,
        w_out,
        b_out,
        gain_one,
        shift_one,
        w_in,
        b_in,
        w_down,
        b_down,
        gain_two,
        shift_two,
    ) = args
    slots, rows, width = tokens.shape
    pairs = width // WIDE
    position = lax.axis_index("fsdp")
    deal_row = deal[0]
    my_lengths = lax.dynamic_slice_in_dim(lengths[0], position * slots, slots)
    spots = jnp.arange(deal_row.shape[0], dtype=jnp.int32)
    inverse = jnp.sum(
        jnp.where(deal_row[None, :] == spots[:, None], spots[None, :], 0), axis=1
    )

    singles = (b_query, b_value, b_out, gain_one, shift_one, b_in, b_down, gain_two, shift_two)
    own, up_own = join(w_query, w_key, w_value, w_out, w_in)
    first = Gather(grid, own)
    up_weights = Gather(grid, up_own)
    down_weights = Gather(grid, w_down)

    got = first.send_line()
    got_up = up_weights.send_line()
    got_down = down_weights.send_line()
    first.take_line(got)
    got = first.send_plane()
    singles, first.held = tie(singles, first.held)
    small = jnp.concatenate(singles)
    small = lax.all_to_all(
        jnp.broadcast_to(small[None, :], (grid.total, small.shape[0])), BOTH, 0, 0, tiled=True
    )
    (cotangent, got), _ = tie((cotangent, got), ())
    first.take_plane(got)
    up_weights.take_line(got_up)
    down_weights.take_line(got_down)
    (up_weights.held, down_weights.held), _ = tie(
        (up_weights.held, down_weights.held), got
    )
    got = first.send_core()
    got_up = up_weights.send_plane()
    up_spread = spread_out(cotangent)
    qkv = first.whole(got)

    vectors = []
    at = 0
    for one in singles:
        vectors.append(small[:, at : at + one.shape[0]].reshape(-1).astype(f32))
        at += one.shape[0]
    bq, bv, bo, g1, s1, bi, bd, g2, s2 = vectors

    total_rows = slots * rows
    inputs = tokens.reshape(total_rows, width)
    valid = jnp.arange(rows)[None, :] < my_lengths[:, None]
    valid_row = valid.reshape(total_rows)[:, None]

    bias = interleave(bq[None], jnp.zeros_like(bq)[None], bv[None])
    fused = (matmul(inputs, qkv) + bias).astype(bf16)
    (down_weights.held, fused) = lax.optimization_barrier((down_weights.held, fused))
    got_down = down_weights.send_plane()
    halves = []
    for slot in range(slots):
        halves.append(attend(fused, my_lengths, slots, slot, 1))
        (fused, halves), _ = tie((fused, halves), ())
    (halves, up_spread), got_up = tie((halves, up_spread), got_up)
    up_weights.take_plane(got_up)
    got_up = up_weights.send_core()
    upstream = bring_in(up_spread, deal_row)
    context = jnp.concatenate([half[0] for half in halves], axis=0)
    totals = jnp.concatenate([half[1] for half in halves], axis=0)
    up_whole = up_weights.whole(got_up)
    wo, wi = up_whole[:, :width], up_whole[:, width:]

    middle_norm, middle_spread = standardize(inputs.astype(f32) + matmul(context, wo) + bo)
    middle = middle_norm * g1 + s1
    middle_low = middle.astype(bf16)
    hidden = matmul(middle_low, wi) + bi
    active = gelu_value(hidden).astype(bf16)
    active, got_down = tie(active, got_down)
    down_weights.take_plane(got_down)
    wd = down_weights.whole(down_weights.send_core())
    final_norm, final_spread = standardize(middle + matmul(active, wd) + bd)
    output = jnp.where(valid_row, final_norm * g2 + s2, 0.0).astype(bf16)

    upstream = joined(upstream).reshape(total_rows, width).astype(f32)
    d_result = jnp.where(valid_row, upstream, 0.0)
    grad_g2 = jnp.sum(d_result * final_norm, axis=0)
    grad_s2 = jnp.sum(d_result, axis=0)
    d_final = norm_back(d_result * g2, final_norm, final_spread)
    d_branch = d_final.astype(bf16)
    grad_bd = jnp.sum(d_branch.astype(f32), axis=0)

    plane, line = ("y", "x"), ("zh", "zl")
    sum_down, sum_up, sum_first, sum_second = (Scatter(grid) for _ in range(4))
    other = grad_tall(grid, active, d_branch, 1)
    got_down = sum_down.send_core(other)
    own_down = grad_tall(grid, active, d_branch, 0)
    output, d_branch = tie(output, d_branch)
    out_spread = spread_out(output.reshape(slots, rows, width))
    d_hidden = (right_times(d_branch, wd) * gelu_slope(hidden)).astype(bf16)
    grad_bi = jnp.sum(d_hidden.astype(f32), axis=0)
    d_hidden, got_down = tie(d_hidden, got_down)
    got_down = sum_down.send_plane(own_down, got_down)
    own_up, other = grad_wide(grid, middle_low, d_hidden)
    got_up = sum_up.send_core(other)
    d_middle = d_final + right_times(d_hidden, wi)
    grad_g1 = jnp.sum(d_middle * middle_norm, axis=0)
    grad_s1 = jnp.sum(d_middle, axis=0)
    d_sum = norm_back(d_middle * g1, middle_norm, middle_spread)
    d_attended = d_sum.astype(bf16)
    grad_bo = jnp.sum(d_attended.astype(f32), axis=0)
    d_attended, got_up = tie(d_attended, got_up)
    got_up = sum_up.send_plane(own_up, got_up)
    half = pairs // 2
    wide = width + half * 3 * WIDE
    begun = grad_wide(grid, context, d_attended, wide)
    d_context = right_times(d_attended, wo).astype(bf16)
    d_first, sums_first = attend_back(fused, totals, d_context, my_lengths, slots, 0, half)
    (d_first, d_context, out_spread), got_down = tie((d_first, d_context, out_spread), got_down)
    got_down = sum_down.send_line(got_down)
    out_pieces = bring_in(out_spread, inverse)
    own_first, other = grad_wide(grid, inputs, d_first, wide, width, begun)
    got_first = sum_first.send_core(other)
    d_second, sums_second = attend_back(
        fused, totals, d_context, my_lengths, slots, half, pairs - half
    )
    (d_second, d_sum), (got_up, got_first) = tie((d_second, d_sum), (got_up, got_first))
    got_first = sum_first.send_plane(own_first, got_first)
    own_second, other = grad_wide(grid, inputs, d_second)
    got_second = sum_second.send_core(other)
    got_up = sum_up.send_line(got_up)
    d_fused = jnp.concatenate([d_first, d_second], axis=1)
    (d_fused, d_sum), got_second = tie((d_fused, d_sum), got_second)
    got_second = sum_second.send_plane(own_second, got_second)
    input_grad = (d_sum + right_times(d_fused, qkv)).astype(bf16).reshape(slots, rows, width)
    input_grad, got_first = tie(input_grad, got_first)
    got_first = sum_first.send_line(got_first)
    got_second = sum_second.send_line(got_second)
    shard_first = sum_first.finish(got_first)
    shard_second = sum_second.finish(got_second)
    layer_out = joined(out_pieces)
    shard_qkv = jnp.concatenate([shard_first[:, width:], shard_second], axis=1).reshape(-1, pairs, 3, WIDE)
    shard_q, shard_k, shard_v = (shard_qkv[:, :, i].reshape(-1, width) for i in range(3))
    sums = jnp.sum(jnp.concatenate([sums_first, sums_second], axis=-1), axis=0)

    grads = (sums[0], sums[1], grad_bo, grad_g1, grad_s1, grad_bi, grad_bd, grad_g2, grad_s2)
    small = jnp.concatenate([one.reshape(grid.total, -1) for one in grads], axis=1)
    small = jnp.sum(lax.all_to_all(small, BOTH, 0, 0, tiled=True), axis=0)
    parts = []
    at = 0
    for one in singles:
        parts.append(small[at : at + one.shape[0]])
        at += one.shape[0]
    pbq, pbv, pbo, pg1, ps1, pbi, pbd, pg2, ps2 = parts
    return (
        layer_out,
        input_grad,
        shard_q,
        pbq,
        shard_k,
        shard_v,
        pbv,
        shard_first[:, :width],
        pbo,
        pg1,
        ps1,
        sum_up.finish(got_up),
        pbi,
        sum_down.finish(got_down),
        pbd,
        pg2,
        ps2,
    )


def solution(mesh):
    grid = Grid(mesh)
    rows3 = P(BOTH, None, None)
    rows2 = P(BOTH, None)
    rows1 = P(BOTH)
    table = P("dp", None)
    kinds = (2, 1, 2, 2, 1, 2, 1, 1, 1, 2, 1, 2, 1, 1, 1)
    placed = tuple(rows2 if kind == 2 else rows1 for kind in kinds)

    def step(*args):
        return per_device(grid, *args)

    return jax.shard_map(
        step,
        mesh=mesh,
        in_specs=(rows3, rows3, table, table) + placed,
        out_specs=(rows3, rows3) + placed,
        check_vma=False,
    )
```

```python
import itertools

import jax
import jax.numpy as jnp
from jax import lax
from jax.experimental import pallas as pl
from jax.experimental.pallas import tpu as pltpu
from jax.sharding import PartitionSpec as P

HD = 64
WIDE = 2 * HD
NEG = -1e30
LINE = 4
BOTH = ("dp", "fsdp")
bf16 = jnp.bfloat16
f32 = jnp.float32

norm_eps = 1e-12
half_root = 0.7071067811865476
slope_scale = 0.3989422804014327


class Grid:
    def __init__(self, mesh):
        self.dp = mesh.shape["dp"]
        self.fsdp = mesh.shape["fsdp"]
        self.total = self.dp * self.fsdp
        nx = self.fsdp // LINE
        ny = self.dp // 2
        self.size = {"y": ny, "core": 2, "zh": 2, "zl": 2, "x": nx}
        self.stride = {"x": 1, "zl": nx, "zh": 2 * nx, "core": self.fsdp, "y": 2 * self.fsdp}

    def place(self, axis):
        me = lax.axis_index("dp") * self.fsdp + lax.axis_index("fsdp")
        return (me // self.stride[axis]) % self.size[axis]

    def spot(self):
        line = self.place("zh") * 2 + self.place("zl")
        return jnp.stack([self.place("y"), self.place("core"), line, self.place("x")]).astype(
            jnp.int32
        )

    def swap(self, array, axis, step):
        mask = self.stride[axis] * step
        return lax.ppermute(array, BOTH, [(i, i ^ mask) for i in range(self.total)])


AXES = ("y", "core", "zh", "zl", "x")


def place_kernel(spot, *refs, keys):
    out = refs[-1]
    for part, (y, core, x) in zip(refs, keys):
        out[spot[0] ^ y, spot[1] ^ core, 0, spot[3] ^ x] = part[0]


class Gather:
    def __init__(self, grid, shard):
        self.grid = grid
        self.held = shard

    def fetch(self, array, **steps):
        grid = self.grid
        mask = sum(grid.stride[axis] * step for axis, step in steps.items())
        return lax.ppermute(array, BOTH, [(k, k ^ mask) for k in range(grid.total)])

    def send_line(self):
        return [self.fetch(self.held, zl=step & 1, zh=step >> 1) for step in range(1, LINE)]

    def take_line(self, got):
        parts = [self.held] + list(got)
        me = self.grid.place("zh") * 2 + self.grid.place("zl")
        shape = (LINE,) + self.held.shape
        line = lax.broadcasted_iota(jnp.int32, shape, 0)
        held = parts[-1][None]
        for step in range(LINE - 2, -1, -1):
            held = jnp.where(line == (me ^ step), parts[step][None], held)
        self.held = held

    def send_plane(self):
        sizes = self.grid.size
        self.keys = [(y, x) for y in range(sizes["y"]) for x in range(sizes["x"])]
        return [self.fetch(self.held, y=y, x=x) for y, x in self.keys[1:]]

    def take_plane(self, got):
        self.parts = [self.held] + list(got)

    def send_core(self):
        return [self.fetch(part, core=1) for part in self.parts]

    def whole(self, got):
        grid = self.grid
        rows, wide = self.held.shape[1:]
        keys = [(y, core, x) for core in range(2) for y, x in self.keys]
        shape = (grid.size["y"], 2, LINE, grid.size["x"], rows, wide)
        out = pl.pallas_call(
            lambda *refs: place_kernel(*refs, keys=keys),
            grid_spec=pltpu.PrefetchScalarGridSpec(
                num_scalar_prefetch=1,
                grid=(LINE,),
                in_specs=[pl.BlockSpec((1, rows, wide), lambda i, _: (i, 0, 0))] * len(keys),
                out_specs=pl.BlockSpec(
                    shape[:2] + (1,) + shape[3:], lambda i, _: (0, 0, i, 0, 0, 0)
                ),
            ),
            out_shape=jax.ShapeDtypeStruct(shape, bf16),
            cost_estimate=pl.CostEstimate(
                flops=0, bytes_accessed=4 * grid.total * rows * wide, transcendentals=0
            ),
            name="place",
        )(grid.spot(), *self.parts, *got)
        return out.reshape(grid.total * rows, wide)


def join_kernel(query_ref, key_ref, value_ref, out_ref, in_ref, down_ref, first_ref, up_ref):
    rows, width = out_ref.shape
    for pair in range(width // WIDE):
        for i, ref in enumerate((query_ref, key_ref, value_ref)):
            at = (pair * 3 + i) * WIDE
            first_ref[:, at : at + WIDE] = ref[:, pair * WIDE : (pair + 1) * WIDE]
    for i in range(down_ref.shape[0] // rows):
        up_ref[:, i * width : (i + 1) * width] = down_ref[i * rows : (i + 1) * rows, :]
    at = in_ref.shape[1]
    up_ref[:, at : at + width] = out_ref[...]
    up_ref[:, at + width :] = in_ref[...]


def join(w_query, w_key, w_value, w_out, w_in, w_down):
    rows, width = w_query.shape
    return pl.pallas_call(
        join_kernel,
        out_shape=[
            jax.ShapeDtypeStruct((rows, 3 * width), bf16),
            jax.ShapeDtypeStruct((rows, width + 2 * w_in.shape[1]), bf16),
        ],
        name="join",
    )(w_query, w_key, w_value, w_out, w_in, w_down)


def stack_kernel(wide_ref, out_ref):
    count, rows, wide = wide_ref.shape
    width = out_ref.shape[1]
    folds = wide // width
    for k in range(count):
        for i in range(folds):
            at = (k * folds + i) * rows
            out_ref[at : at + rows, :] = wide_ref[k, :, i * width : (i + 1) * width]


def stack(gathered, total, width):
    rows = gathered.shape[0] // total
    wide = (gathered.shape[1] - width) // 2
    folds = wide // width
    count = 4
    return pl.pallas_call(
        stack_kernel,
        grid=(total // count,),
        in_specs=[pl.BlockSpec((count, rows, wide), lambda i: (i, 0, 0))],
        out_specs=pl.BlockSpec((count * folds * rows, width), lambda i: (i, 0)),
        out_shape=jax.ShapeDtypeStruct((total * folds * rows, width), bf16),
        cost_estimate=pl.CostEstimate(
            flops=0, bytes_accessed=4 * total * rows * wide, transcendentals=0
        ),
        name="stack",
    )(gathered.reshape(total, rows, -1))


STRIP = 512
SLAB = 384


def grad_down_kernel(left_ref, right_ref, out_ref, *, rows):
    total = tn(left_ref[...], right_ref[...]).astype(bf16)
    tall, width = total.shape
    folds = out_ref.shape[1] // width
    for k in range(tall // rows):
        at = k // folds * rows
        fold = k % folds
        out_ref[at : at + rows, fold * width : (fold + 1) * width] = total[k * rows : (k + 1) * rows]


def grad_down(grid, left, right):
    count, tall = left.shape
    width = right.shape[1]
    rows = width // grid.total
    return pl.pallas_call(
        lambda *refs: grad_down_kernel(*refs, rows=rows),
        grid=(tall // SLAB,),
        in_specs=[
            pl.BlockSpec((count, SLAB), lambda i: (0, i)),
            pl.BlockSpec((count, width), lambda i: (0, 0)),
        ],
        out_specs=pl.BlockSpec((SLAB * width // tall, tall), lambda i: (i, 0)),
        out_shape=jax.ShapeDtypeStruct((width, 2 * tall), bf16),
        cost_estimate=pl.CostEstimate(
            flops=0, bytes_accessed=4 * width, transcendentals=0
        ),
        name="grad_down",
    )(left, right)


def grad_up_kernel(left_ref, right_ref, _, out_ref, turned):
    @pl.when(pl.program_id(0) == 0)
    def _():
        turned[...] = left_ref[...].T

    out_ref[...] = jnp.dot(turned[...], right_ref[...], preferred_element_type=f32).astype(bf16)


def grad_up(left, right, base):
    rows, tall = left.shape
    wide = right.shape[1]
    at = wide // STRIP
    return pl.pallas_call(
        grad_up_kernel,
        grid=(wide // STRIP,),
        in_specs=[
            pl.BlockSpec((rows, tall), lambda j: (0, 0)),
            pl.BlockSpec((rows, STRIP), lambda j: (0, j)),
            pl.BlockSpec(memory_space=pl.ANY),
        ],
        out_specs=pl.BlockSpec((tall, STRIP), lambda j: (0, j + at)),
        scratch_shapes=[pltpu.VMEM((tall, rows), bf16)],
        out_shape=jax.ShapeDtypeStruct(base.shape, bf16),
        input_output_aliases={2: 0},
        cost_estimate=pl.CostEstimate(
            flops=0, bytes_accessed=4 * wide, transcendentals=0
        ),
        name="grad_up",
    )(left, right, base)


def fold_plane_kernel(spot, *refs, keys, widths):
    count = len(widths)
    owns, gots, outs = refs[:count], refs[count : 2 * count], refs[2 * count :]
    for out, (y, x) in zip(outs, keys):
        at = (spot[0] ^ y, 0, spot[3] ^ x)
        left = 0
        for own, got, wide in zip(owns, gots, widths):
            out[0, :, left : left + wide] = (
                own[at].astype(f32) + got[at].astype(f32)
            ).astype(bf16)
            left += wide


def fold_line_kernel(spot, *refs, counts):
    outs = refs[-LINE:]
    for step, out in enumerate(outs):
        at = left = 0
        for count in counts:
            parts = refs[at : at + count]
            total = parts[0][spot[2] ^ step].astype(f32)
            for part in parts[1:]:
                total = total + part[spot[2] ^ step].astype(f32)
            wide = total.shape[1]
            out[:, left : left + wide] = total.astype(bf16)
            at += count
            left += wide


class Scatter:
    def __init__(self, grid):
        self.grid = grid

    def fetch(self, array, **steps):
        grid = self.grid
        mask = sum(grid.stride[axis] * step for axis, step in steps.items())
        return lax.ppermute(array, BOTH, [(k, k ^ mask) for k in range(grid.total)])

    def send_core(self, others):
        return [self.fetch(other, core=1) for other in others]

    def send_plane(self, owns, gots):
        grid = self.grid
        ny, nx = grid.size["y"], grid.size["x"]
        rows = owns[0].shape[0] // (ny * LINE * nx)
        widths = [own.shape[1] for own in owns]
        wide = sum(widths)
        keys = [(y, x) for y in range(ny) for x in range(nx)]
        blocks = [
            pl.BlockSpec((ny, 1, nx, rows, one), lambda i, _: (0, i, 0, 0, 0)) for one in widths
        ]
        parts = pl.pallas_call(
            lambda *refs: fold_plane_kernel(*refs, keys=keys, widths=widths),
            grid_spec=pltpu.PrefetchScalarGridSpec(
                num_scalar_prefetch=1,
                grid=(LINE,),
                in_specs=blocks + blocks,
                out_specs=[pl.BlockSpec((1, rows, wide), lambda i, _: (i, 0, 0))] * len(keys),
            ),
            out_shape=[jax.ShapeDtypeStruct((LINE, rows, wide), bf16)] * len(keys),
            cost_estimate=pl.CostEstimate(
                flops=0, bytes_accessed=6 * owns[0].shape[0] * wide, transcendentals=0
            ),
            name="fold_plane",
        )(grid.spot(), *[one.reshape(ny, LINE, nx, rows, -1) for one in (*owns, *gots)])
        return [parts[0]] + [self.fetch(part, y=y, x=x) for part, (y, x) in zip(parts[1:], keys[1:])]

    def send_line(self, groups):
        rows = groups[0][0].shape[1]
        widths = [group[0].shape[2] for group in groups]
        wide = sum(widths)
        counts = [len(group) for group in groups]
        parts = pl.pallas_call(
            lambda *refs: fold_line_kernel(*refs, counts=counts),
            grid_spec=pltpu.PrefetchScalarGridSpec(
                num_scalar_prefetch=1,
                grid=(1,),
                in_specs=[
                    pl.BlockSpec((LINE, rows, one), lambda i, _: (0, 0, 0))
                    for one, count in zip(widths, counts)
                    for _ in range(count)
                ],
                out_specs=[pl.BlockSpec((rows, wide), lambda i, _: (0, 0))] * LINE,
            ),
            out_shape=[jax.ShapeDtypeStruct((rows, wide), bf16)] * LINE,
            cost_estimate=pl.CostEstimate(
                flops=0, bytes_accessed=8 * LINE * rows * wide, transcendentals=0
            ),
            name="fold_line",
        )(self.grid.spot(), *[part for group in groups for part in group])
        return [parts[0]] + [
            self.fetch(part, zl=step & 1, zh=step >> 1)
            for step, part in zip(range(1, LINE), parts[1:])
        ]

    def finish(self, parts):
        total = parts[0].astype(f32)
        for one in parts[1:]:
            total = total + one.astype(f32)
        return total


def turn(grid, array):
    rows, tall = array.shape
    turned = array.T.reshape(grid.size["y"], 2, -1, rows)
    core = grid.place("core")
    return [
        lax.dynamic_index_in_dim(turned, at, 1, keepdims=False).reshape(-1, rows)
        for at in (core, 1 - core)
    ]


def gate(*values):
    return lax.optimization_barrier(values)


def standardize(values):
    centre = values - jnp.mean(values, axis=-1, keepdims=True)
    spread = lax.rsqrt(jnp.mean(centre * centre, axis=-1, keepdims=True) + norm_eps)
    return (centre * spread, spread)


def norm_back(d_normed, normed, spread):
    return spread * (
        d_normed
        - jnp.mean(d_normed, axis=-1, keepdims=True)
        - normed * jnp.mean(d_normed * normed, axis=-1, keepdims=True)
    )


def gelu_value(values):
    return 0.5 * values * (1.0 + lax.erf(values * half_root))


def gelu_slope(values):
    return (
        0.5 * (1.0 + lax.erf(values * half_root))
        + values * jnp.exp(-0.5 * values * values) * slope_scale
    )


def matmul(left, right):
    return jnp.dot(left, right, preferred_element_type=f32)


def left_times(left, right):
    return jnp.einsum("ti,to->io", left, right, preferred_element_type=f32)


def right_times(grads, weight):
    return jnp.einsum("to,io->ti", grads, weight, preferred_element_type=f32)


def nt(left, right):
    return lax.dot_general(left, right, (((1,), (1,)), ((), ())), preferred_element_type=f32)


def tn(left, right):
    return lax.dot_general(left, right, (((0,), (0,)), ((), ())), preferred_element_type=f32)


def head_lanes(shape, head):
    lane = lax.broadcasted_iota(jnp.int32, shape, 1)
    return (lane >= head * HD) & (lane < (head + 1) * HD)


def score_operands(query, key_rows, length, head):
    rows, wide = query.shape
    lane = lax.broadcasted_iota(jnp.int32, (rows, wide), 1)
    row = lax.broadcasted_iota(jnp.int32, (rows, wide), 0)
    spare = (1 - head) * HD
    mine = head_lanes((rows, wide), head)
    one = jnp.where(lane == spare, 1.0, 0.0).astype(bf16)
    mask = jnp.where(row < length, 0.0, NEG).astype(bf16)
    left = jnp.where(mine, query * bf16(HD ** (-0.5)), one)
    right = jnp.where(lane == spare, mask, key_rows)
    return left, right


def attend_kernel(lengths, fused_ref, context_ref, total_ref, *, first):
    length = lengths[first + pl.program_id(0)]
    query, key_rows, value = (fused_ref[:, i * WIDE : (i + 1) * WIDE] for i in range(3))
    weights, values, scales = [], [], []
    for head in range(2):
        left, right = score_operands(query, key_rows, length, head)
        scores = nt(right, left)
        top = jnp.max(scores, axis=0, keepdims=True)
        raised = jnp.exp(scores - top)
        amount = jnp.sum(raised, axis=0, keepdims=True)
        total_ref[0, 0, head : head + 1, :] = top + jnp.log(amount)
        scales.append(1.0 / amount)
        weights.append(raised.astype(bf16))
        values.append(jnp.where(head_lanes(value.shape, head), value, bf16(0)))
    context = tn(jnp.concatenate(values, axis=0), jnp.concatenate(weights, axis=0))
    context = jnp.concatenate([context[:HD] * scales[0], context[HD:] * scales[1]], axis=0)
    context_ref[...] = context.T.astype(bf16)


def attend(fused, lengths, slots, first, count):
    width = fused.shape[1] // 3
    rows = fused.shape[0] // slots
    pairs = width // WIDE
    return pl.pallas_call(
        lambda *refs: attend_kernel(*refs, first=first),
        grid_spec=pltpu.PrefetchScalarGridSpec(
            num_scalar_prefetch=1,
            grid=(count, pairs),
            in_specs=[pl.BlockSpec((rows, 3 * WIDE), lambda s, h, _: (s + first, h))],
            out_specs=[
                pl.BlockSpec((rows, WIDE), lambda s, h, _: (s, h)),
                pl.BlockSpec((1, 1, 2, rows), lambda s, h, _: (s, h, 0, 0)),
            ],
        ),
        out_shape=[
            jax.ShapeDtypeStruct((count * rows, width), bf16),
            jax.ShapeDtypeStruct((count, pairs, 2, rows), f32),
        ],
        cost_estimate=pl.CostEstimate(
            flops=4 * count * rows * rows * width * 4,
            bytes_accessed=8 * count * rows * width,
            transcendentals=count * pairs * 2 * rows * rows,
        ),
        name="attend",
    )(lengths, fused)


def attend_back_kernel(lengths, fused_ref, total_ref, up_ref, d_ref, sums_ref):
    length = lengths[pl.program_id(1)]
    query, key_rows, value = (fused_ref[:, i * WIDE : (i + 1) * WIDE] for i in range(3))
    up = up_ref[...]
    weights, slopes, ups, queries, keys = [], [], [], [], []
    for head in range(2):
        left, right = score_operands(query, key_rows, length, head)
        mine = head_lanes(query.shape, head)
        scores = nt(right, left)
        probs = jnp.exp(scores - total_ref[0, 0, head : head + 1, :])
        masked = jnp.where(mine, up, bf16(0))
        d_probs = nt(value, masked)
        product = probs * d_probs
        d_scores = product - probs * jnp.sum(product, axis=0, keepdims=True)
        weights.append(probs.astype(bf16))
        slopes.append(d_scores.astype(bf16))
        ups.append(masked)
        queries.append(jnp.where(mine, query * bf16(HD ** (-0.5)), bf16(0)))
        keys.append(jnp.where(mine, key_rows * bf16(HD ** (-0.5)), bf16(0)))
    d_value = jnp.dot(
        jnp.concatenate(weights, axis=1), jnp.concatenate(ups, axis=0), preferred_element_type=f32
    ).astype(bf16)
    d_key = jnp.dot(
        jnp.concatenate(slopes, axis=1), jnp.concatenate(queries, axis=0), preferred_element_type=f32
    ).astype(bf16)
    d_query = tn(jnp.concatenate(keys, axis=0), jnp.concatenate(slopes, axis=0)).T.astype(bf16)
    d_ref[:, 0:WIDE] = d_query
    d_ref[:, WIDE : 2 * WIDE] = d_key
    d_ref[:, 2 * WIDE :] = d_value
    sums_ref[0, 0:1, :] = jnp.sum(d_query.astype(f32), axis=0, keepdims=True)
    sums_ref[0, 1:2, :] = jnp.sum(d_value.astype(f32), axis=0, keepdims=True)


def attend_back(fused, totals, up, lengths, slots, first, count):
    width = fused.shape[1] // 3
    rows = fused.shape[0] // slots
    return pl.pallas_call(
        attend_back_kernel,
        grid_spec=pltpu.PrefetchScalarGridSpec(
            num_scalar_prefetch=1,
            grid=(count, slots),
            in_specs=[
                pl.BlockSpec((rows, 3 * WIDE), lambda h, s, _: (s, first + h)),
                pl.BlockSpec((1, 1, 2, rows), lambda h, s, _: (s, first + h, 0, 0)),
                pl.BlockSpec((rows, WIDE), lambda h, s, _: (s, first + h)),
            ],
            out_specs=[
                pl.BlockSpec((rows, 3 * WIDE), lambda h, s, _: (s, h)),
                pl.BlockSpec((1, 2, WIDE), lambda h, s, _: (s, 0, h)),
            ],
        ),
        out_shape=[
            jax.ShapeDtypeStruct((slots * rows, count * 3 * WIDE), bf16),
            jax.ShapeDtypeStruct((slots, 2, count * WIDE), f32),
        ],
        cost_estimate=pl.CostEstimate(
            flops=10 * slots * rows * rows * count * WIDE * 4,
            bytes_accessed=16 * slots * rows * count * WIDE,
            transcendentals=slots * count * 2 * rows * rows,
        ),
        name="attend_back",
    )(lengths, fused, totals, up)


def interleave(query, key_rows, value):
    lead = query.shape[0]
    return jnp.stack([one.reshape(lead, -1, WIDE) for one in (query, key_rows, value)], axis=2).reshape(
        lead, -1
    )


def pieces_out(array, count):
    slots, rows, width = array.shape
    return array.reshape(slots, count, rows // count, width).transpose(1, 0, 2, 3)


def spread_out(array):
    count = lax.axis_size("fsdp")
    return lax.all_to_all(pieces_out(array, count), "fsdp", 0, 0, tiled=True)


def bring_in(spread, source):
    count, slots, short, width = spread.shape
    spread = spread.reshape(count * slots, short, width)
    spread = jnp.take(spread, source, axis=0, mode="clip").reshape(count, slots, short, width)
    return lax.all_to_all(spread, "fsdp", 0, 0, tiled=True)


def joined(pieces):
    count, slots, short, width = pieces.shape
    return pieces.transpose(1, 0, 2, 3).reshape(slots, count * short, width)


def per_device(grid, *args):
    (
        tokens,
        cotangent,
        lengths,
        deal,
        w_query,
        b_query,
        w_key,
        w_value,
        b_value,
        w_out,
        b_out,
        gain_one,
        shift_one,
        w_in,
        b_in,
        w_down,
        b_down,
        gain_two,
        shift_two,
    ) = args
    slots, rows, width = tokens.shape
    pairs = width // WIDE
    position = lax.axis_index("fsdp")
    deal_row = deal[0]
    my_lengths = lax.dynamic_slice_in_dim(lengths[0], position * slots, slots)
    spots = jnp.arange(deal_row.shape[0], dtype=jnp.int32)
    inverse = jnp.sum(
        jnp.where(deal_row[None, :] == spots[:, None], spots[None, :], 0), axis=1
    )

    singles = (b_query, b_value, b_out, gain_one, shift_one, b_in, b_down, gain_two, shift_two)
    own, up_own = join(w_query, w_key, w_value, w_out, w_in, w_down)
    first = Gather(grid, own)
    got = first.send_line()
    up_whole = lax.all_gather(up_own, BOTH, axis=0, tiled=True)
    small = jnp.concatenate(singles)
    small = jnp.broadcast_to(small[None, :], (grid.total, small.shape[0]))
    cut = pieces_out(cotangent, lax.axis_size("fsdp"))

    got, small, cut = gate(got, small, cut)
    first.take_line(got)
    got = first.send_plane()
    small = lax.all_to_all(small, BOTH, 0, 0, tiled=True)

    tokens_own, tokens_other = turn(grid, tokens.reshape(slots * rows, width))
    got, small, tokens_own, tokens_other = gate(got, small, tokens_own, tokens_other)
    first.take_plane(got)
    got = first.send_core()
    up_spread = lax.all_to_all(cut, "fsdp", 0, 0, tiled=True)
    vectors = []
    at = 0
    for one in singles:
        vectors.append(small[:, at : at + one.shape[0]].reshape(-1).astype(f32))
        at += one.shape[0]
    bq, bv, bo, g1, s1, bi, bd, g2, s2 = vectors
    bias = interleave(bq[None], jnp.zeros_like(bq)[None], bv[None])

    got, bias, tokens = gate(got, bias, tokens)
    qkv = first.whole(got)

    total_rows = slots * rows
    inputs = tokens.reshape(total_rows, width)
    valid = jnp.arange(rows)[None, :] < my_lengths[:, None]
    valid_row = valid.reshape(total_rows)[:, None]

    fused = (matmul(inputs, qkv) + bias).astype(bf16)
    halves = [attend(fused, my_lengths, slots, 0, 1)]
    for slot in range(1, slots):
        halves.append(attend(fused, my_lengths, slots, slot, 1))
    halves, up_spread = gate(halves, up_spread)
    context = jnp.concatenate([half[0] for half in halves], axis=0)
    totals = jnp.concatenate([half[1] for half in halves], axis=0)
    context_own, context_other = turn(grid, context)
    upstream = bring_in(up_spread, deal_row)
    context, context_own, context_other, up_whole = gate(
        context, context_own, context_other, up_whole
    )
    tall = w_in.shape[1]
    wo, wi = up_whole[:, tall : tall + width], up_whole[:, tall + width :]
    wd = stack(up_whole, grid.total, width)

    middle_norm, middle_spread = standardize(inputs.astype(f32) + matmul(context, wo) + bo)
    middle = middle_norm * g1 + s1
    middle_low = middle.astype(bf16)
    hidden = matmul(middle_low, wi) + bi
    active = gelu_value(hidden).astype(bf16)
    final_norm, final_spread = standardize(middle + matmul(active, wd) + bd)
    output = jnp.where(valid_row, final_norm * g2 + s2, 0.0).astype(bf16)
    output, upstream = gate(output, upstream)

    upstream = joined(upstream).reshape(total_rows, width).astype(f32)
    d_result = jnp.where(valid_row, upstream, 0.0)
    grad_g2 = jnp.sum(d_result * final_norm, axis=0)
    grad_s2 = jnp.sum(d_result, axis=0)
    d_final = norm_back(d_result * g2, final_norm, final_spread)
    d_branch = d_final.astype(bf16)
    grad_bd = jnp.sum(d_branch.astype(f32), axis=0)

    scatter = Scatter(grid)
    out_spread = spread_out(output.reshape(slots, rows, width))
    d_branch, grad_g2, grad_s2, grad_bd = gate(d_branch, grad_g2, grad_s2, grad_bd)
    d_hidden = (right_times(d_branch, wd) * gelu_slope(hidden)).astype(bf16)
    grad_bi = jnp.sum(d_hidden.astype(f32), axis=0)
    d_hidden, d_branch = gate(d_hidden, d_branch)
    outer = grad_up(middle_low, d_hidden, grad_down(grid, active, d_branch))
    outer, d_hidden, grad_bi, out_spread = gate(outer, d_hidden, grad_bi, out_spread)
    out_pieces = bring_in(out_spread, inverse)
    shard_outer = lax.psum_scatter(outer, BOTH, scatter_dimension=0, tiled=True)
    d_middle = d_final + right_times(d_hidden, wi)
    grad_g1 = jnp.sum(d_middle * middle_norm, axis=0)
    grad_s1 = jnp.sum(d_middle, axis=0)
    d_sum = norm_back(d_middle * g1, middle_norm, middle_spread)
    d_attended = d_sum.astype(bf16)
    grad_bo = jnp.sum(d_attended.astype(f32), axis=0)
    half = pairs // 2
    d_context = right_times(d_attended, wo).astype(bf16)
    d_first, sums_first = attend_back(fused, totals, d_context, my_lengths, slots, 0, half)
    others = [
        matmul(context_other, d_attended).astype(bf16),
        matmul(tokens_other, d_first).astype(bf16),
    ]
    others, d_context, d_attended, d_first = gate(others, d_context, d_attended, d_first)
    got_first = scatter.send_core(others)
    own_first = [
        matmul(context_own, d_attended).astype(bf16),
        matmul(tokens_own, d_first).astype(bf16),
    ]
    own_first, got_first, d_context, out_pieces = gate(own_first, got_first, d_context, out_pieces)
    got_first = scatter.send_plane(own_first, got_first)
    d_context, got_first[0] = gate(d_context, got_first[0])
    d_second, sums_second = attend_back(
        fused, totals, d_context, my_lengths, slots, half, pairs - half
    )
    other = matmul(tokens_other, d_second).astype(bf16)
    partial = d_sum + right_times(d_first, qkv[:, : half * 3 * WIDE])
    other, d_second, sums_second, partial, got_first = gate(
        other, d_second, sums_second, partial, got_first
    )
    got_second = scatter.send_core([other])
    own_second = matmul(tokens_own, d_second).astype(bf16)
    own_second, d_second, got_second = gate(own_second, d_second, got_second)
    got_second = scatter.send_plane([own_second], got_second)
    got_second[0], d_second, sums_second = gate(got_second[0], d_second, sums_second)
    input_grad = partial + right_times(d_second, qkv[:, half * 3 * WIDE :])
    input_grad = input_grad.astype(bf16).reshape(slots, rows, width)
    sums = jnp.sum(jnp.concatenate([sums_first, sums_second], axis=-1), axis=0)
    input_grad, got_second, got_first = gate(input_grad, got_second, got_first)
    got = scatter.send_line([got_first, got_second])
    shard = scatter.finish(got)
    layer_out = joined(out_pieces)
    shard_qkv = shard[:, width:].reshape(-1, pairs, 3, WIDE)
    shard_down = shard_outer[:, :tall].reshape(shard_outer.shape[0], -1, width).transpose(1, 0, 2)
    shard_q, shard_k, shard_v = (shard_qkv[:, :, i].reshape(-1, width) for i in range(3))

    grads = (sums[0], sums[1], grad_bo, grad_g1, grad_s1, grad_bi, grad_bd, grad_g2, grad_s2)
    small = jnp.concatenate([one.reshape(grid.total, -1) for one in grads], axis=1)
    small = jnp.sum(lax.all_to_all(small, BOTH, 0, 0, tiled=True), axis=0)
    parts = []
    at = 0
    for one in singles:
        parts.append(small[at : at + one.shape[0]])
        at += one.shape[0]
    pbq, pbv, pbo, pg1, ps1, pbi, pbd, pg2, ps2 = parts
    return (
        layer_out,
        input_grad,
        shard_q,
        pbq,
        shard_k,
        shard_v,
        pbv,
        shard[:, :width],
        pbo,
        pg1,
        ps1,
        shard_outer[:, tall:].astype(f32),
        pbi,
        shard_down.astype(f32).reshape(-1, width),
        pbd,
        pg2,
        ps2,
    )


def solution(mesh):
    grid = Grid(mesh)
    rows3 = P(BOTH, None, None)
    rows2 = P(BOTH, None)
    rows1 = P(BOTH)
    table = P("dp", None)
    kinds = (2, 1, 2, 2, 1, 2, 1, 1, 1, 2, 1, 2, 1, 1, 1)
    placed = tuple(rows2 if kind == 2 else rows1 for kind in kinds)

    def step(*args):
        return per_device(grid, *args)

    return jax.shard_map(
        step,
        mesh=mesh,
        in_specs=(rows3, rows3, table, table) + placed,
        out_specs=(rows3, rows3) + placed,
        check_vma=False,
    )
```

```python
import itertools

import jax
import jax.numpy as jnp
from jax import lax
from jax.experimental import pallas as pl
from jax.experimental.pallas import tpu as pltpu
from jax.sharding import PartitionSpec as P

HD = 64
WIDE = 2 * HD
NEG = -1e30
LINE = 4
BOTH = ("dp", "fsdp")
bf16 = jnp.bfloat16
f32 = jnp.float32

norm_eps = 1e-12
half_root = 0.7071067811865476
slope_scale = 0.3989422804014327


class Grid:
    def __init__(self, mesh):
        self.dp = mesh.shape["dp"]
        self.fsdp = mesh.shape["fsdp"]
        self.total = self.dp * self.fsdp
        nx = self.fsdp // LINE
        ny = self.dp // 2
        self.size = {"y": ny, "core": 2, "zh": 2, "zl": 2, "x": nx}
        self.stride = {"x": 1, "zl": nx, "zh": 2 * nx, "core": self.fsdp, "y": 2 * self.fsdp}

    def place(self, axis):
        me = lax.axis_index("dp") * self.fsdp + lax.axis_index("fsdp")
        return (me // self.stride[axis]) % self.size[axis]

    def spot(self):
        line = self.place("zh") * 2 + self.place("zl")
        return jnp.stack([self.place("y"), self.place("core"), line, self.place("x")]).astype(
            jnp.int32
        )

    def swap(self, array, axis, step):
        mask = self.stride[axis] * step
        return lax.ppermute(array, BOTH, [(i, i ^ mask) for i in range(self.total)])


AXES = ("y", "core", "zh", "zl", "x")


def place_kernel(spot, *refs, keys):
    out = refs[-1]
    for part, (y, core, x) in zip(refs, keys):
        out[spot[0] ^ y, spot[1] ^ core, 0, spot[3] ^ x] = part[0]


class Gather:
    def __init__(self, grid, shard):
        self.grid = grid
        self.held = shard

    def fetch(self, array, **steps):
        grid = self.grid
        mask = sum(grid.stride[axis] * step for axis, step in steps.items())
        return lax.ppermute(array, BOTH, [(k, k ^ mask) for k in range(grid.total)])

    def send_line(self):
        return [self.fetch(self.held, zl=step & 1, zh=step >> 1) for step in range(1, LINE)]

    def take_line(self, got):
        parts = [self.held] + list(got)
        me = self.grid.place("zh") * 2 + self.grid.place("zl")
        shape = (LINE,) + self.held.shape
        line = lax.broadcasted_iota(jnp.int32, shape, 0)
        held = parts[-1][None]
        for step in range(LINE - 2, -1, -1):
            held = jnp.where(line == (me ^ step), parts[step][None], held)
        self.held = held

    def send_plane(self):
        sizes = self.grid.size
        self.keys = [(y, x) for y in range(sizes["y"]) for x in range(sizes["x"])]
        return [self.fetch(self.held, y=y, x=x) for y, x in self.keys[1:]]

    def take_plane(self, got):
        self.parts = [self.held] + list(got)

    def send_core(self):
        return [self.fetch(part, core=1) for part in self.parts]

    def whole(self, got):
        grid = self.grid
        rows, wide = self.held.shape[1:]
        keys = [(y, core, x) for core in range(2) for y, x in self.keys]
        shape = (grid.size["y"], 2, LINE, grid.size["x"], rows, wide)
        out = pl.pallas_call(
            lambda *refs: place_kernel(*refs, keys=keys),
            grid_spec=pltpu.PrefetchScalarGridSpec(
                num_scalar_prefetch=1,
                grid=(LINE,),
                in_specs=[pl.BlockSpec((1, rows, wide), lambda i, _: (i, 0, 0))] * len(keys),
                out_specs=pl.BlockSpec(
                    shape[:2] + (1,) + shape[3:], lambda i, _: (0, 0, i, 0, 0, 0)
                ),
            ),
            out_shape=jax.ShapeDtypeStruct(shape, bf16),
            cost_estimate=pl.CostEstimate(
                flops=0, bytes_accessed=4 * grid.total * rows * wide, transcendentals=0
            ),
            name="place",
        )(grid.spot(), *self.parts, *got)
        return out.reshape(grid.total * rows, wide)


def join_kernel(query_ref, key_ref, value_ref, out_ref, in_ref, first_ref, up_ref):
    width = out_ref.shape[1]
    for pair in range(width // WIDE):
        for i, ref in enumerate((query_ref, key_ref, value_ref)):
            at = (pair * 3 + i) * WIDE
            first_ref[:, at : at + WIDE] = ref[:, pair * WIDE : (pair + 1) * WIDE]
    up_ref[:, :width] = out_ref[...]
    up_ref[:, width:] = in_ref[...]


def join(w_query, w_key, w_value, w_out, w_in):
    rows, width = w_query.shape
    return pl.pallas_call(
        join_kernel,
        out_shape=[
            jax.ShapeDtypeStruct((rows, 3 * width), bf16),
            jax.ShapeDtypeStruct((rows, width + w_in.shape[1]), bf16),
        ],
        name="join",
    )(w_query, w_key, w_value, w_out, w_in)


STRIP = 512
SLAB = 384


def grad_down_kernel(left_ref, right_ref, out_ref, *, rows):
    total = tn(left_ref[...], right_ref[...]).astype(bf16)
    tall, width = total.shape
    folds = out_ref.shape[1] // width
    for k in range(tall // rows):
        at = k // folds * rows
        fold = k % folds
        out_ref[at : at + rows, fold * width : (fold + 1) * width] = total[k * rows : (k + 1) * rows]


def grad_down(grid, left, right):
    count, tall = left.shape
    width = right.shape[1]
    rows = width // grid.total
    return pl.pallas_call(
        lambda *refs: grad_down_kernel(*refs, rows=rows),
        grid=(tall // SLAB,),
        in_specs=[
            pl.BlockSpec((count, SLAB), lambda i: (0, i)),
            pl.BlockSpec((count, width), lambda i: (0, 0)),
        ],
        out_specs=pl.BlockSpec((SLAB * width // tall, tall), lambda i: (i, 0)),
        out_shape=jax.ShapeDtypeStruct((width, 2 * tall), bf16),
        cost_estimate=pl.CostEstimate(
            flops=0, bytes_accessed=4 * width, transcendentals=0
        ),
        name="grad_down",
    )(left, right)


def grad_up_kernel(left_ref, right_ref, _, out_ref, turned):
    @pl.when(pl.program_id(0) == 0)
    def _():
        turned[...] = left_ref[...].T

    out_ref[...] = jnp.dot(turned[...], right_ref[...], preferred_element_type=f32).astype(bf16)


def grad_up(left, right, base):
    rows, tall = left.shape
    wide = right.shape[1]
    at = wide // STRIP
    return pl.pallas_call(
        grad_up_kernel,
        grid=(wide // STRIP,),
        in_specs=[
            pl.BlockSpec((rows, tall), lambda j: (0, 0)),
            pl.BlockSpec((rows, STRIP), lambda j: (0, j)),
            pl.BlockSpec(memory_space=pl.ANY),
        ],
        out_specs=pl.BlockSpec((tall, STRIP), lambda j: (0, j + at)),
        scratch_shapes=[pltpu.VMEM((tall, rows), bf16)],
        out_shape=jax.ShapeDtypeStruct(base.shape, bf16),
        input_output_aliases={2: 0},
        cost_estimate=pl.CostEstimate(
            flops=0, bytes_accessed=4 * wide, transcendentals=0
        ),
        name="grad_up",
    )(left, right, base)


def fold_plane_kernel(spot, *refs, keys, widths):
    count = len(widths)
    owns, gots, outs = refs[:count], refs[count : 2 * count], refs[2 * count :]
    for out, (y, x) in zip(outs, keys):
        at = (spot[0] ^ y, 0, spot[3] ^ x)
        left = 0
        for own, got, wide in zip(owns, gots, widths):
            out[0, :, left : left + wide] = (
                own[at].astype(f32) + got[at].astype(f32)
            ).astype(bf16)
            left += wide


def fold_line_kernel(spot, *refs, counts):
    outs = refs[-LINE:]
    for step, out in enumerate(outs):
        at = left = 0
        for count in counts:
            parts = refs[at : at + count]
            total = parts[0][spot[2] ^ step].astype(f32)
            for part in parts[1:]:
                total = total + part[spot[2] ^ step].astype(f32)
            wide = total.shape[1]
            out[:, left : left + wide] = total.astype(bf16)
            at += count
            left += wide


class Scatter:
    def __init__(self, grid):
        self.grid = grid

    def fetch(self, array, **steps):
        grid = self.grid
        mask = sum(grid.stride[axis] * step for axis, step in steps.items())
        return lax.ppermute(array, BOTH, [(k, k ^ mask) for k in range(grid.total)])

    def send_core(self, others):
        return [self.fetch(other, core=1) for other in others]

    def send_plane(self, owns, gots):
        grid = self.grid
        ny, nx = grid.size["y"], grid.size["x"]
        rows = owns[0].shape[0] // (ny * LINE * nx)
        widths = [own.shape[1] for own in owns]
        wide = sum(widths)
        keys = [(y, x) for y in range(ny) for x in range(nx)]
        blocks = [
            pl.BlockSpec((ny, 1, nx, rows, one), lambda i, _: (0, i, 0, 0, 0)) for one in widths
        ]
        parts = pl.pallas_call(
            lambda *refs: fold_plane_kernel(*refs, keys=keys, widths=widths),
            grid_spec=pltpu.PrefetchScalarGridSpec(
                num_scalar_prefetch=1,
                grid=(LINE,),
                in_specs=blocks + blocks,
                out_specs=[pl.BlockSpec((1, rows, wide), lambda i, _: (i, 0, 0))] * len(keys),
            ),
            out_shape=[jax.ShapeDtypeStruct((LINE, rows, wide), bf16)] * len(keys),
            cost_estimate=pl.CostEstimate(
                flops=0, bytes_accessed=6 * owns[0].shape[0] * wide, transcendentals=0
            ),
            name="fold_plane",
        )(grid.spot(), *[one.reshape(ny, LINE, nx, rows, -1) for one in (*owns, *gots)])
        return [parts[0]] + [self.fetch(part, y=y, x=x) for part, (y, x) in zip(parts[1:], keys[1:])]

    def send_line(self, groups):
        rows = groups[0][0].shape[1]
        widths = [group[0].shape[2] for group in groups]
        wide = sum(widths)
        counts = [len(group) for group in groups]
        parts = pl.pallas_call(
            lambda *refs: fold_line_kernel(*refs, counts=counts),
            grid_spec=pltpu.PrefetchScalarGridSpec(
                num_scalar_prefetch=1,
                grid=(1,),
                in_specs=[
                    pl.BlockSpec((LINE, rows, one), lambda i, _: (0, 0, 0))
                    for one, count in zip(widths, counts)
                    for _ in range(count)
                ],
                out_specs=[pl.BlockSpec((rows, wide), lambda i, _: (0, 0))] * LINE,
            ),
            out_shape=[jax.ShapeDtypeStruct((rows, wide), bf16)] * LINE,
            cost_estimate=pl.CostEstimate(
                flops=0, bytes_accessed=8 * LINE * rows * wide, transcendentals=0
            ),
            name="fold_line",
        )(self.grid.spot(), *[part for group in groups for part in group])
        return [parts[0]] + [
            self.fetch(part, zl=step & 1, zh=step >> 1)
            for step, part in zip(range(1, LINE), parts[1:])
        ]

    def finish(self, parts):
        total = parts[0].astype(f32)
        for one in parts[1:]:
            total = total + one.astype(f32)
        return total


def turn(grid, array):
    rows, tall = array.shape
    turned = array.T.reshape(grid.size["y"], 2, -1, rows)
    core = grid.place("core")
    return [
        lax.dynamic_index_in_dim(turned, at, 1, keepdims=False).reshape(-1, rows)
        for at in (core, 1 - core)
    ]


def gate(*values):
    return lax.optimization_barrier(values)


def standardize(values):
    centre = values - jnp.mean(values, axis=-1, keepdims=True)
    spread = lax.rsqrt(jnp.mean(centre * centre, axis=-1, keepdims=True) + norm_eps)
    return (centre * spread, spread)


def norm_back(d_normed, normed, spread):
    return spread * (
        d_normed
        - jnp.mean(d_normed, axis=-1, keepdims=True)
        - normed * jnp.mean(d_normed * normed, axis=-1, keepdims=True)
    )


def gelu_value(values):
    return 0.5 * values * (1.0 + lax.erf(values * half_root))


def gelu_slope(values):
    return (
        0.5 * (1.0 + lax.erf(values * half_root))
        + values * jnp.exp(-0.5 * values * values) * slope_scale
    )


def matmul(left, right):
    return jnp.dot(left, right, preferred_element_type=f32)


def left_times(left, right):
    return jnp.einsum("ti,to->io", left, right, preferred_element_type=f32)


def right_times(grads, weight):
    return jnp.einsum("to,io->ti", grads, weight, preferred_element_type=f32)


def nt(left, right):
    return lax.dot_general(left, right, (((1,), (1,)), ((), ())), preferred_element_type=f32)


def tn(left, right):
    return lax.dot_general(left, right, (((0,), (0,)), ((), ())), preferred_element_type=f32)


def head_lanes(shape, head):
    lane = lax.broadcasted_iota(jnp.int32, shape, 1)
    return (lane >= head * HD) & (lane < (head + 1) * HD)


def score_operands(query, key_rows, length, head):
    rows, wide = query.shape
    lane = lax.broadcasted_iota(jnp.int32, (rows, wide), 1)
    row = lax.broadcasted_iota(jnp.int32, (rows, wide), 0)
    spare = (1 - head) * HD
    mine = head_lanes((rows, wide), head)
    one = jnp.where(lane == spare, 1.0, 0.0).astype(bf16)
    mask = jnp.where(row < length, 0.0, NEG).astype(bf16)
    left = jnp.where(mine, query * bf16(HD ** (-0.5)), one)
    right = jnp.where(lane == spare, mask, key_rows)
    return left, right


def attend_kernel(lengths, fused_ref, context_ref, total_ref, *, first):
    length = lengths[first + pl.program_id(0)]
    query, key_rows, value = (fused_ref[:, i * WIDE : (i + 1) * WIDE] for i in range(3))
    weights, values, scales = [], [], []
    for head in range(2):
        left, right = score_operands(query, key_rows, length, head)
        scores = nt(right, left)
        top = jnp.max(scores, axis=0, keepdims=True)
        raised = jnp.exp(scores - top)
        amount = jnp.sum(raised, axis=0, keepdims=True)
        total_ref[0, 0, head : head + 1, :] = top + jnp.log(amount)
        scales.append(1.0 / amount)
        weights.append(raised.astype(bf16))
        values.append(jnp.where(head_lanes(value.shape, head), value, bf16(0)))
    context = tn(jnp.concatenate(values, axis=0), jnp.concatenate(weights, axis=0))
    context = jnp.concatenate([context[:HD] * scales[0], context[HD:] * scales[1]], axis=0)
    context_ref[...] = context.T.astype(bf16)


def attend(fused, lengths, slots, first, count):
    width = fused.shape[1] // 3
    rows = fused.shape[0] // slots
    pairs = width // WIDE
    return pl.pallas_call(
        lambda *refs: attend_kernel(*refs, first=first),
        grid_spec=pltpu.PrefetchScalarGridSpec(
            num_scalar_prefetch=1,
            grid=(count, pairs),
            in_specs=[pl.BlockSpec((rows, 3 * WIDE), lambda s, h, _: (s + first, h))],
            out_specs=[
                pl.BlockSpec((rows, WIDE), lambda s, h, _: (s, h)),
                pl.BlockSpec((1, 1, 2, rows), lambda s, h, _: (s, h, 0, 0)),
            ],
        ),
        out_shape=[
            jax.ShapeDtypeStruct((count * rows, width), bf16),
            jax.ShapeDtypeStruct((count, pairs, 2, rows), f32),
        ],
        cost_estimate=pl.CostEstimate(
            flops=4 * count * rows * rows * width * 4,
            bytes_accessed=8 * count * rows * width,
            transcendentals=count * pairs * 2 * rows * rows,
        ),
        name="attend",
    )(lengths, fused)


def attend_back_kernel(lengths, fused_ref, total_ref, up_ref, d_ref, sums_ref):
    length = lengths[pl.program_id(1)]
    query, key_rows, value = (fused_ref[:, i * WIDE : (i + 1) * WIDE] for i in range(3))
    up = up_ref[...]
    weights, slopes, ups, queries, keys = [], [], [], [], []
    for head in range(2):
        left, right = score_operands(query, key_rows, length, head)
        mine = head_lanes(query.shape, head)
        scores = nt(right, left)
        probs = jnp.exp(scores - total_ref[0, 0, head : head + 1, :])
        masked = jnp.where(mine, up, bf16(0))
        d_probs = nt(value, masked)
        product = probs * d_probs
        d_scores = product - probs * jnp.sum(product, axis=0, keepdims=True)
        weights.append(probs.astype(bf16))
        slopes.append(d_scores.astype(bf16))
        ups.append(masked)
        queries.append(jnp.where(mine, query * bf16(HD ** (-0.5)), bf16(0)))
        keys.append(jnp.where(mine, key_rows * bf16(HD ** (-0.5)), bf16(0)))
    d_value = jnp.dot(
        jnp.concatenate(weights, axis=1), jnp.concatenate(ups, axis=0), preferred_element_type=f32
    ).astype(bf16)
    d_key = jnp.dot(
        jnp.concatenate(slopes, axis=1), jnp.concatenate(queries, axis=0), preferred_element_type=f32
    ).astype(bf16)
    d_query = tn(jnp.concatenate(keys, axis=0), jnp.concatenate(slopes, axis=0)).T.astype(bf16)
    d_ref[:, 0:WIDE] = d_query
    d_ref[:, WIDE : 2 * WIDE] = d_key
    d_ref[:, 2 * WIDE :] = d_value
    sums_ref[0, 0:1, :] = jnp.sum(d_query.astype(f32), axis=0, keepdims=True)
    sums_ref[0, 1:2, :] = jnp.sum(d_value.astype(f32), axis=0, keepdims=True)


def attend_back(fused, totals, up, lengths, slots, first, count):
    width = fused.shape[1] // 3
    rows = fused.shape[0] // slots
    return pl.pallas_call(
        attend_back_kernel,
        grid_spec=pltpu.PrefetchScalarGridSpec(
            num_scalar_prefetch=1,
            grid=(count, slots),
            in_specs=[
                pl.BlockSpec((rows, 3 * WIDE), lambda h, s, _: (s, first + h)),
                pl.BlockSpec((1, 1, 2, rows), lambda h, s, _: (s, first + h, 0, 0)),
                pl.BlockSpec((rows, WIDE), lambda h, s, _: (s, first + h)),
            ],
            out_specs=[
                pl.BlockSpec((rows, 3 * WIDE), lambda h, s, _: (s, h)),
                pl.BlockSpec((1, 2, WIDE), lambda h, s, _: (s, 0, h)),
            ],
        ),
        out_shape=[
            jax.ShapeDtypeStruct((slots * rows, count * 3 * WIDE), bf16),
            jax.ShapeDtypeStruct((slots, 2, count * WIDE), f32),
        ],
        cost_estimate=pl.CostEstimate(
            flops=10 * slots * rows * rows * count * WIDE * 4,
            bytes_accessed=16 * slots * rows * count * WIDE,
            transcendentals=slots * count * 2 * rows * rows,
        ),
        name="attend_back",
    )(lengths, fused, totals, up)


def interleave(query, key_rows, value):
    lead = query.shape[0]
    return jnp.stack([one.reshape(lead, -1, WIDE) for one in (query, key_rows, value)], axis=2).reshape(
        lead, -1
    )


def pieces_out(array, count):
    slots, rows, width = array.shape
    return array.reshape(slots, count, rows // count, width).transpose(1, 0, 2, 3)


def spread_out(array):
    count = lax.axis_size("fsdp")
    return lax.all_to_all(pieces_out(array, count), "fsdp", 0, 0, tiled=True)


def bring_in(spread, source):
    count, slots, short, width = spread.shape
    spread = spread.reshape(count * slots, short, width)
    spread = jnp.take(spread, source, axis=0, mode="clip").reshape(count, slots, short, width)
    return lax.all_to_all(spread, "fsdp", 0, 0, tiled=True)


def joined(pieces):
    count, slots, short, width = pieces.shape
    return pieces.transpose(1, 0, 2, 3).reshape(slots, count * short, width)


def per_device(grid, *args):
    (
        tokens,
        cotangent,
        lengths,
        deal,
        w_query,
        b_query,
        w_key,
        w_value,
        b_value,
        w_out,
        b_out,
        gain_one,
        shift_one,
        w_in,
        b_in,
        w_down,
        b_down,
        gain_two,
        shift_two,
    ) = args
    slots, rows, width = tokens.shape
    pairs = width // WIDE
    position = lax.axis_index("fsdp")
    deal_row = deal[0]
    my_lengths = lax.dynamic_slice_in_dim(lengths[0], position * slots, slots)
    spots = jnp.arange(deal_row.shape[0], dtype=jnp.int32)
    inverse = jnp.sum(
        jnp.where(deal_row[None, :] == spots[:, None], spots[None, :], 0), axis=1
    )

    singles = (b_query, b_value, b_out, gain_one, shift_one, b_in, b_down, gain_two, shift_two)
    own, up_own = join(w_query, w_key, w_value, w_out, w_in)
    first = Gather(grid, own)
    got = first.send_line()
    up_whole = lax.all_gather(up_own, BOTH, axis=0, tiled=True)
    small = jnp.concatenate(singles)
    small = jnp.broadcast_to(small[None, :], (grid.total, small.shape[0]))
    cut = pieces_out(cotangent, lax.axis_size("fsdp"))

    got, small, cut, w_down = gate(got, small, cut, w_down)
    first.take_line(got)
    got = first.send_plane()
    down_weights = Gather(grid, w_down)
    got_down = down_weights.send_line()
    small = lax.all_to_all(small, BOTH, 0, 0, tiled=True)

    tokens_own, tokens_other = turn(grid, tokens.reshape(slots * rows, width))
    got, got_down, small, cut, tokens_own, tokens_other = gate(
        got, got_down, small, cut, tokens_own, tokens_other
    )
    first.take_plane(got)
    got = first.send_core()
    down_weights.take_line(got_down)
    got_down = down_weights.send_plane()
    up_spread = lax.all_to_all(cut, "fsdp", 0, 0, tiled=True)
    vectors = []
    at = 0
    for one in singles:
        vectors.append(small[:, at : at + one.shape[0]].reshape(-1).astype(f32))
        at += one.shape[0]
    bq, bv, bo, g1, s1, bi, bd, g2, s2 = vectors
    bias = interleave(bq[None], jnp.zeros_like(bq)[None], bv[None])

    got, bias, tokens = gate(got, bias, tokens)
    qkv = first.whole(got)

    total_rows = slots * rows
    inputs = tokens.reshape(total_rows, width)
    valid = jnp.arange(rows)[None, :] < my_lengths[:, None]
    valid_row = valid.reshape(total_rows)[:, None]

    fused = (matmul(inputs, qkv) + bias).astype(bf16)
    halves = [attend(fused, my_lengths, slots, 0, 1)]
    for slot in range(1, slots):
        halves.append(attend(fused, my_lengths, slots, slot, 1))
    context = jnp.concatenate([half[0] for half in halves], axis=0)
    totals = jnp.concatenate([half[1] for half in halves], axis=0)
    context_own, context_other = turn(grid, context)
    context, context_own, context_other, up_whole = gate(
        context, context_own, context_other, up_whole
    )
    wo, wi = up_whole[:, :width], up_whole[:, width:]
    tall = w_in.shape[1]

    middle_norm, middle_spread = standardize(inputs.astype(f32) + matmul(context, wo) + bo)
    middle = middle_norm * g1 + s1
    middle_low = middle.astype(bf16)
    middle_low, got_down, up_spread = gate(middle_low, got_down, up_spread)
    down_weights.take_plane(got_down)
    got_down = down_weights.send_core()
    upstream = bring_in(up_spread, deal_row)
    hidden = matmul(middle_low, wi) + bi
    active = gelu_value(hidden).astype(bf16)
    active, got_down = gate(active, got_down)
    wd = down_weights.whole(got_down)
    final_norm, final_spread = standardize(middle + matmul(active, wd) + bd)
    output = jnp.where(valid_row, final_norm * g2 + s2, 0.0).astype(bf16)
    output, upstream = gate(output, upstream)

    upstream = joined(upstream).reshape(total_rows, width).astype(f32)
    d_result = jnp.where(valid_row, upstream, 0.0)
    grad_g2 = jnp.sum(d_result * final_norm, axis=0)
    grad_s2 = jnp.sum(d_result, axis=0)
    d_final = norm_back(d_result * g2, final_norm, final_spread)
    d_branch = d_final.astype(bf16)
    grad_bd = jnp.sum(d_branch.astype(f32), axis=0)

    scatter = Scatter(grid)
    out_spread = spread_out(output.reshape(slots, rows, width))
    d_branch, grad_g2, grad_s2, grad_bd = gate(d_branch, grad_g2, grad_s2, grad_bd)
    d_hidden = (right_times(d_branch, wd) * gelu_slope(hidden)).astype(bf16)
    grad_bi = jnp.sum(d_hidden.astype(f32), axis=0)
    d_hidden, d_branch = gate(d_hidden, d_branch)
    outer = grad_up(middle_low, d_hidden, grad_down(grid, active, d_branch))
    outer, d_hidden, grad_bi, out_spread = gate(outer, d_hidden, grad_bi, out_spread)
    out_pieces = bring_in(out_spread, inverse)
    shard_outer = lax.psum_scatter(outer, BOTH, scatter_dimension=0, tiled=True)
    d_middle = d_final + right_times(d_hidden, wi)
    grad_g1 = jnp.sum(d_middle * middle_norm, axis=0)
    grad_s1 = jnp.sum(d_middle, axis=0)
    d_sum = norm_back(d_middle * g1, middle_norm, middle_spread)
    d_attended = d_sum.astype(bf16)
    grad_bo = jnp.sum(d_attended.astype(f32), axis=0)
    half = pairs // 2
    d_context = right_times(d_attended, wo).astype(bf16)
    d_first, sums_first = attend_back(fused, totals, d_context, my_lengths, slots, 0, half)
    others = [
        matmul(context_other, d_attended).astype(bf16),
        matmul(tokens_other, d_first).astype(bf16),
    ]
    others, d_context, d_attended, d_first = gate(others, d_context, d_attended, d_first)
    got_first = scatter.send_core(others)
    own_first = [
        matmul(context_own, d_attended).astype(bf16),
        matmul(tokens_own, d_first).astype(bf16),
    ]
    own_first, got_first, d_context, out_pieces = gate(own_first, got_first, d_context, out_pieces)
    got_first = scatter.send_plane(own_first, got_first)
    d_context, got_first[0] = gate(d_context, got_first[0])
    d_second, sums_second = attend_back(
        fused, totals, d_context, my_lengths, slots, half, pairs - half
    )
    other = matmul(tokens_other, d_second).astype(bf16)
    partial = d_sum + right_times(d_first, qkv[:, : half * 3 * WIDE])
    other, d_second, sums_second, partial, got_first = gate(
        other, d_second, sums_second, partial, got_first
    )
    got_second = scatter.send_core([other])
    own_second = matmul(tokens_own, d_second).astype(bf16)
    own_second, d_second, got_second = gate(own_second, d_second, got_second)
    got_second = scatter.send_plane([own_second], got_second)
    got_second[0], d_second, sums_second = gate(got_second[0], d_second, sums_second)
    input_grad = partial + right_times(d_second, qkv[:, half * 3 * WIDE :])
    input_grad = input_grad.astype(bf16).reshape(slots, rows, width)
    sums = jnp.sum(jnp.concatenate([sums_first, sums_second], axis=-1), axis=0)
    input_grad, got_second, got_first = gate(input_grad, got_second, got_first)
    got = scatter.send_line([got_first, got_second])
    shard = scatter.finish(got)
    layer_out = joined(out_pieces)
    shard_qkv = shard[:, width:].reshape(-1, pairs, 3, WIDE)
    shard_down = shard_outer[:, :tall].reshape(shard_outer.shape[0], -1, width).transpose(1, 0, 2)
    shard_q, shard_k, shard_v = (shard_qkv[:, :, i].reshape(-1, width) for i in range(3))

    grads = (sums[0], sums[1], grad_bo, grad_g1, grad_s1, grad_bi, grad_bd, grad_g2, grad_s2)
    small = jnp.concatenate([one.reshape(grid.total, -1) for one in grads], axis=1)
    small = jnp.sum(lax.all_to_all(small, BOTH, 0, 0, tiled=True), axis=0)
    parts = []
    at = 0
    for one in singles:
        parts.append(small[at : at + one.shape[0]])
        at += one.shape[0]
    pbq, pbv, pbo, pg1, ps1, pbi, pbd, pg2, ps2 = parts
    return (
        layer_out,
        input_grad,
        shard_q,
        pbq,
        shard_k,
        shard_v,
        pbv,
        shard[:, :width],
        pbo,
        pg1,
        ps1,
        shard_outer[:, tall:].astype(f32),
        pbi,
        shard_down.astype(f32).reshape(-1, width),
        pbd,
        pg2,
        ps2,
    )


def solution(mesh):
    grid = Grid(mesh)
    rows3 = P(BOTH, None, None)
    rows2 = P(BOTH, None)
    rows1 = P(BOTH)
    table = P("dp", None)
    kinds = (2, 1, 2, 2, 1, 2, 1, 1, 1, 2, 1, 2, 1, 1, 1)
    placed = tuple(rows2 if kind == 2 else rows1 for kind in kinds)

    def step(*args):
        return per_device(grid, *args)

    return jax.shard_map(
        step,
        mesh=mesh,
        in_specs=(rows3, rows3, table, table) + placed,
        out_specs=(rows3, rows3) + placed,
        check_vma=False,
    )
```

```python
import itertools

import jax
import jax.numpy as jnp
from jax import lax
from jax.experimental import pallas as pl
from jax.experimental.pallas import tpu as pltpu
from jax.sharding import PartitionSpec as P

HD = 64
WIDE = 2 * HD
NEG = -1e30
LINE = 4
BOTH = ("dp", "fsdp")
bf16 = jnp.bfloat16
f32 = jnp.float32

norm_eps = 1e-12
half_root = 0.7071067811865476
slope_scale = 0.3989422804014327


class Grid:
    def __init__(self, mesh):
        self.dp = mesh.shape["dp"]
        self.fsdp = mesh.shape["fsdp"]
        self.total = self.dp * self.fsdp
        nx = self.fsdp // LINE
        ny = self.dp // 2
        self.size = {"y": ny, "core": 2, "zh": 2, "zl": 2, "x": nx}
        self.stride = {"x": 1, "zl": nx, "zh": 2 * nx, "core": self.fsdp, "y": 2 * self.fsdp}

    def place(self, axis):
        me = lax.axis_index("dp") * self.fsdp + lax.axis_index("fsdp")
        return (me // self.stride[axis]) % self.size[axis]

    def spot(self):
        line = self.place("zh") * 2 + self.place("zl")
        return jnp.stack([self.place("y"), self.place("core"), line, self.place("x")]).astype(
            jnp.int32
        )

    def swap(self, array, axis, step):
        mask = self.stride[axis] * step
        return lax.ppermute(array, BOTH, [(i, i ^ mask) for i in range(self.total)])


AXES = ("y", "core", "zh", "zl", "x")


def place_kernel(spot, *refs, keys):
    out = refs[-1]
    for part, (y, core, x) in zip(refs, keys):
        out[spot[0] ^ y, spot[1] ^ core, 0, spot[3] ^ x] = part[0]


class Gather:
    def __init__(self, grid, shard):
        self.grid = grid
        self.held = shard

    def fetch(self, array, **steps):
        grid = self.grid
        mask = sum(grid.stride[axis] * step for axis, step in steps.items())
        return lax.ppermute(array, BOTH, [(k, k ^ mask) for k in range(grid.total)])

    def send_line(self):
        return [self.fetch(self.held, zl=step & 1, zh=step >> 1) for step in range(1, LINE)]

    def take_line(self, got):
        parts = [self.held] + list(got)
        me = self.grid.place("zh") * 2 + self.grid.place("zl")
        shape = (LINE,) + self.held.shape
        line = lax.broadcasted_iota(jnp.int32, shape, 0)
        held = parts[-1][None]
        for step in range(LINE - 2, -1, -1):
            held = jnp.where(line == (me ^ step), parts[step][None], held)
        self.held = held

    def send_plane(self):
        sizes = self.grid.size
        self.keys = [(y, x) for y in range(sizes["y"]) for x in range(sizes["x"])]
        return [self.fetch(self.held, y=y, x=x) for y, x in self.keys[1:]]

    def take_plane(self, got):
        self.parts = [self.held] + list(got)

    def send_core(self):
        return [self.fetch(part, core=1) for part in self.parts]

    def whole(self, got):
        grid = self.grid
        rows, wide = self.held.shape[1:]
        keys = [(y, core, x) for core in range(2) for y, x in self.keys]
        shape = (grid.size["y"], 2, LINE, grid.size["x"], rows, wide)
        out = pl.pallas_call(
            lambda *refs: place_kernel(*refs, keys=keys),
            grid_spec=pltpu.PrefetchScalarGridSpec(
                num_scalar_prefetch=1,
                grid=(LINE,),
                in_specs=[pl.BlockSpec((1, rows, wide), lambda i, _: (i, 0, 0))] * len(keys),
                out_specs=pl.BlockSpec(
                    shape[:2] + (1,) + shape[3:], lambda i, _: (0, 0, i, 0, 0, 0)
                ),
            ),
            out_shape=jax.ShapeDtypeStruct(shape, bf16),
            cost_estimate=pl.CostEstimate(
                flops=0, bytes_accessed=4 * grid.total * rows * wide, transcendentals=0
            ),
            name="place",
        )(grid.spot(), *self.parts, *got)
        return out.reshape(grid.total * rows, wide)


def join_kernel(query_ref, key_ref, value_ref, out_ref, in_ref, first_ref, up_ref):
    width = out_ref.shape[1]
    for pair in range(width // WIDE):
        for i, ref in enumerate((query_ref, key_ref, value_ref)):
            at = (pair * 3 + i) * WIDE
            first_ref[:, at : at + WIDE] = ref[:, pair * WIDE : (pair + 1) * WIDE]
    up_ref[:, :width] = out_ref[...]
    up_ref[:, width:] = in_ref[...]


def join(w_query, w_key, w_value, w_out, w_in):
    rows, width = w_query.shape
    return pl.pallas_call(
        join_kernel,
        out_shape=[
            jax.ShapeDtypeStruct((rows, 3 * width), bf16),
            jax.ShapeDtypeStruct((rows, width + w_in.shape[1]), bf16),
        ],
        name="join",
    )(w_query, w_key, w_value, w_out, w_in)


STRIP = 512
SLAB = 384


def grad_down_kernel(left_ref, right_ref, out_ref, *, rows):
    total = tn(left_ref[...], right_ref[...]).astype(bf16)
    tall, width = total.shape
    folds = out_ref.shape[1] // width
    for k in range(tall // rows):
        at = k // folds * rows
        fold = k % folds
        out_ref[at : at + rows, fold * width : (fold + 1) * width] = total[k * rows : (k + 1) * rows]


def grad_down(grid, left, right):
    count, tall = left.shape
    width = right.shape[1]
    rows = width // grid.total
    return pl.pallas_call(
        lambda *refs: grad_down_kernel(*refs, rows=rows),
        grid=(tall // SLAB,),
        in_specs=[
            pl.BlockSpec((count, SLAB), lambda i: (0, i)),
            pl.BlockSpec((count, width), lambda i: (0, 0)),
        ],
        out_specs=pl.BlockSpec((SLAB * width // tall, tall), lambda i: (i, 0)),
        out_shape=jax.ShapeDtypeStruct((width, 2 * tall), bf16),
        cost_estimate=pl.CostEstimate(
            flops=0, bytes_accessed=4 * width, transcendentals=0
        ),
        name="grad_down",
    )(left, right)


def grad_up_kernel(left_ref, right_ref, _, out_ref, turned):
    @pl.when(pl.program_id(0) == 0)
    def _():
        turned[...] = left_ref[...].T

    out_ref[...] = jnp.dot(turned[...], right_ref[...], preferred_element_type=f32).astype(bf16)


def grad_up(left, right, base):
    rows, tall = left.shape
    wide = right.shape[1]
    at = wide // STRIP
    return pl.pallas_call(
        grad_up_kernel,
        grid=(wide // STRIP,),
        in_specs=[
            pl.BlockSpec((rows, tall), lambda j: (0, 0)),
            pl.BlockSpec((rows, STRIP), lambda j: (0, j)),
            pl.BlockSpec(memory_space=pl.ANY),
        ],
        out_specs=pl.BlockSpec((tall, STRIP), lambda j: (0, j + at)),
        scratch_shapes=[pltpu.VMEM((tall, rows), bf16)],
        out_shape=jax.ShapeDtypeStruct(base.shape, bf16),
        input_output_aliases={2: 0},
        cost_estimate=pl.CostEstimate(
            flops=0, bytes_accessed=4 * wide, transcendentals=0
        ),
        name="grad_up",
    )(left, right, base)


def fold_plane_kernel(spot, *refs, keys, widths):
    count = len(widths)
    owns, gots, outs = refs[:count], refs[count : 2 * count], refs[2 * count :]
    for out, (y, x) in zip(outs, keys):
        at = (spot[0] ^ y, 0, spot[3] ^ x)
        left = 0
        for own, got, wide in zip(owns, gots, widths):
            out[0, :, left : left + wide] = (
                own[at].astype(f32) + got[at].astype(f32)
            ).astype(bf16)
            left += wide


def fold_line_kernel(spot, *refs, counts):
    outs = refs[-LINE:]
    for step, out in enumerate(outs):
        at = left = 0
        for count in counts:
            parts = refs[at : at + count]
            total = parts[0][spot[2] ^ step].astype(f32)
            for part in parts[1:]:
                total = total + part[spot[2] ^ step].astype(f32)
            wide = total.shape[1]
            out[:, left : left + wide] = total.astype(bf16)
            at += count
            left += wide


class Scatter:
    def __init__(self, grid):
        self.grid = grid

    def fetch(self, array, **steps):
        grid = self.grid
        mask = sum(grid.stride[axis] * step for axis, step in steps.items())
        return lax.ppermute(array, BOTH, [(k, k ^ mask) for k in range(grid.total)])

    def send_core(self, others):
        return [self.fetch(other, core=1) for other in others]

    def send_plane(self, owns, gots):
        grid = self.grid
        ny, nx = grid.size["y"], grid.size["x"]
        rows = owns[0].shape[0] // (ny * LINE * nx)
        widths = [own.shape[1] for own in owns]
        wide = sum(widths)
        keys = [(y, x) for y in range(ny) for x in range(nx)]
        blocks = [
            pl.BlockSpec((ny, 1, nx, rows, one), lambda i, _: (0, i, 0, 0, 0)) for one in widths
        ]
        parts = pl.pallas_call(
            lambda *refs: fold_plane_kernel(*refs, keys=keys, widths=widths),
            grid_spec=pltpu.PrefetchScalarGridSpec(
                num_scalar_prefetch=1,
                grid=(LINE,),
                in_specs=blocks + blocks,
                out_specs=[pl.BlockSpec((1, rows, wide), lambda i, _: (i, 0, 0))] * len(keys),
            ),
            out_shape=[jax.ShapeDtypeStruct((LINE, rows, wide), bf16)] * len(keys),
            cost_estimate=pl.CostEstimate(
                flops=0, bytes_accessed=6 * owns[0].shape[0] * wide, transcendentals=0
            ),
            name="fold_plane",
        )(grid.spot(), *[one.reshape(ny, LINE, nx, rows, -1) for one in (*owns, *gots)])
        return [parts[0]] + [self.fetch(part, y=y, x=x) for part, (y, x) in zip(parts[1:], keys[1:])]

    def send_line(self, groups):
        rows = groups[0][0].shape[1]
        widths = [group[0].shape[2] for group in groups]
        wide = sum(widths)
        counts = [len(group) for group in groups]
        parts = pl.pallas_call(
            lambda *refs: fold_line_kernel(*refs, counts=counts),
            grid_spec=pltpu.PrefetchScalarGridSpec(
                num_scalar_prefetch=1,
                grid=(1,),
                in_specs=[
                    pl.BlockSpec((LINE, rows, one), lambda i, _: (0, 0, 0))
                    for one, count in zip(widths, counts)
                    for _ in range(count)
                ],
                out_specs=[pl.BlockSpec((rows, wide), lambda i, _: (0, 0))] * LINE,
            ),
            out_shape=[jax.ShapeDtypeStruct((rows, wide), bf16)] * LINE,
            cost_estimate=pl.CostEstimate(
                flops=0, bytes_accessed=8 * LINE * rows * wide, transcendentals=0
            ),
            name="fold_line",
        )(self.grid.spot(), *[part for group in groups for part in group])
        return [parts[0]] + [
            self.fetch(part, zl=step & 1, zh=step >> 1)
            for step, part in zip(range(1, LINE), parts[1:])
        ]

    def finish(self, parts):
        total = parts[0].astype(f32)
        for one in parts[1:]:
            total = total + one.astype(f32)
        return total


def turn(grid, array):
    rows, tall = array.shape
    turned = array.T.reshape(grid.size["y"], 2, -1, rows)
    core = grid.place("core")
    return [
        lax.dynamic_index_in_dim(turned, at, 1, keepdims=False).reshape(-1, rows)
        for at in (core, 1 - core)
    ]


def gate(*values):
    return lax.optimization_barrier(values)


def standardize(values):
    centre = values - jnp.mean(values, axis=-1, keepdims=True)
    spread = lax.rsqrt(jnp.mean(centre * centre, axis=-1, keepdims=True) + norm_eps)
    return (centre * spread, spread)


def norm_back(d_normed, normed, spread):
    return spread * (
        d_normed
        - jnp.mean(d_normed, axis=-1, keepdims=True)
        - normed * jnp.mean(d_normed * normed, axis=-1, keepdims=True)
    )


def gelu_value(values):
    return 0.5 * values * (1.0 + lax.erf(values * half_root))


def gelu_slope(values):
    return (
        0.5 * (1.0 + lax.erf(values * half_root))
        + values * jnp.exp(-0.5 * values * values) * slope_scale
    )


def matmul(left, right):
    return jnp.dot(left, right, preferred_element_type=f32)


def left_times(left, right):
    return jnp.einsum("ti,to->io", left, right, preferred_element_type=f32)


def right_times(grads, weight):
    return jnp.einsum("to,io->ti", grads, weight, preferred_element_type=f32)


def nt(left, right):
    return lax.dot_general(left, right, (((1,), (1,)), ((), ())), preferred_element_type=f32)


def tn(left, right):
    return lax.dot_general(left, right, (((0,), (0,)), ((), ())), preferred_element_type=f32)


def head_lanes(shape, head):
    lane = lax.broadcasted_iota(jnp.int32, shape, 1)
    return (lane >= head * HD) & (lane < (head + 1) * HD)


def score_operands(query, key_rows, length, head):
    rows, wide = query.shape
    lane = lax.broadcasted_iota(jnp.int32, (rows, wide), 1)
    row = lax.broadcasted_iota(jnp.int32, (rows, wide), 0)
    spare = (1 - head) * HD
    mine = head_lanes((rows, wide), head)
    one = jnp.where(lane == spare, 1.0, 0.0).astype(bf16)
    mask = jnp.where(row < length, 0.0, NEG).astype(bf16)
    left = jnp.where(mine, query * bf16(HD ** (-0.5)), one)
    right = jnp.where(lane == spare, mask, key_rows)
    return left, right


def attend_kernel(lengths, fused_ref, context_ref, total_ref, *, first):
    length = lengths[first + pl.program_id(0)]
    query, key_rows, value = (fused_ref[:, i * WIDE : (i + 1) * WIDE] for i in range(3))
    weights, values, scales = [], [], []
    for head in range(2):
        left, right = score_operands(query, key_rows, length, head)
        scores = nt(right, left)
        top = jnp.max(scores, axis=0, keepdims=True)
        raised = jnp.exp(scores - top)
        amount = jnp.sum(raised, axis=0, keepdims=True)
        total_ref[0, 0, head : head + 1, :] = top + jnp.log(amount)
        scales.append(1.0 / amount)
        weights.append(raised.astype(bf16))
        values.append(jnp.where(head_lanes(value.shape, head), value, bf16(0)))
    context = tn(jnp.concatenate(values, axis=0), jnp.concatenate(weights, axis=0))
    context = jnp.concatenate([context[:HD] * scales[0], context[HD:] * scales[1]], axis=0)
    context_ref[...] = context.T.astype(bf16)


def attend(fused, lengths, slots, first, count):
    width = fused.shape[1] // 3
    rows = fused.shape[0] // slots
    pairs = width // WIDE
    return pl.pallas_call(
        lambda *refs: attend_kernel(*refs, first=first),
        grid_spec=pltpu.PrefetchScalarGridSpec(
            num_scalar_prefetch=1,
            grid=(count, pairs),
            in_specs=[pl.BlockSpec((rows, 3 * WIDE), lambda s, h, _: (s + first, h))],
            out_specs=[
                pl.BlockSpec((rows, WIDE), lambda s, h, _: (s, h)),
                pl.BlockSpec((1, 1, 2, rows), lambda s, h, _: (s, h, 0, 0)),
            ],
        ),
        out_shape=[
            jax.ShapeDtypeStruct((count * rows, width), bf16),
            jax.ShapeDtypeStruct((count, pairs, 2, rows), f32),
        ],
        cost_estimate=pl.CostEstimate(
            flops=4 * count * rows * rows * width * 4,
            bytes_accessed=8 * count * rows * width,
            transcendentals=count * pairs * 2 * rows * rows,
        ),
        name="attend",
    )(lengths, fused)


def attend_back_kernel(lengths, fused_ref, total_ref, up_ref, d_ref, sums_ref):
    length = lengths[pl.program_id(1)]
    query, key_rows, value = (fused_ref[:, i * WIDE : (i + 1) * WIDE] for i in range(3))
    up = up_ref[...]
    weights, slopes, ups, queries, keys = [], [], [], [], []
    for head in range(2):
        left, right = score_operands(query, key_rows, length, head)
        mine = head_lanes(query.shape, head)
        scores = nt(right, left)
        probs = jnp.exp(scores - total_ref[0, 0, head : head + 1, :])
        masked = jnp.where(mine, up, bf16(0))
        d_probs = nt(value, masked)
        product = probs * d_probs
        d_scores = product - probs * jnp.sum(product, axis=0, keepdims=True)
        weights.append(probs.astype(bf16))
        slopes.append(d_scores.astype(bf16))
        ups.append(masked)
        queries.append(jnp.where(mine, query * bf16(HD ** (-0.5)), bf16(0)))
        keys.append(jnp.where(mine, key_rows * bf16(HD ** (-0.5)), bf16(0)))
    d_value = jnp.dot(
        jnp.concatenate(weights, axis=1), jnp.concatenate(ups, axis=0), preferred_element_type=f32
    ).astype(bf16)
    d_key = jnp.dot(
        jnp.concatenate(slopes, axis=1), jnp.concatenate(queries, axis=0), preferred_element_type=f32
    ).astype(bf16)
    d_query = tn(jnp.concatenate(keys, axis=0), jnp.concatenate(slopes, axis=0)).T.astype(bf16)
    d_ref[:, 0:WIDE] = d_query
    d_ref[:, WIDE : 2 * WIDE] = d_key
    d_ref[:, 2 * WIDE :] = d_value
    sums_ref[0, 0:1, :] = jnp.sum(d_query.astype(f32), axis=0, keepdims=True)
    sums_ref[0, 1:2, :] = jnp.sum(d_value.astype(f32), axis=0, keepdims=True)


def attend_back(fused, totals, up, lengths, slots, first, count):
    width = fused.shape[1] // 3
    rows = fused.shape[0] // slots
    return pl.pallas_call(
        attend_back_kernel,
        grid_spec=pltpu.PrefetchScalarGridSpec(
            num_scalar_prefetch=1,
            grid=(count, slots),
            in_specs=[
                pl.BlockSpec((rows, 3 * WIDE), lambda h, s, meta: (s, meta[slots] + h)),
                pl.BlockSpec((1, 1, 2, rows), lambda h, s, meta: (s, meta[slots] + h, 0, 0)),
                pl.BlockSpec((rows, WIDE), lambda h, s, meta: (s, meta[slots] + h)),
            ],
            out_specs=[
                pl.BlockSpec((rows, 3 * WIDE), lambda h, s, _: (s, h)),
                pl.BlockSpec((1, 2, WIDE), lambda h, s, _: (s, 0, h)),
            ],
        ),
        out_shape=[
            jax.ShapeDtypeStruct((slots * rows, count * 3 * WIDE), bf16),
            jax.ShapeDtypeStruct((slots, 2, count * WIDE), f32),
        ],
        cost_estimate=pl.CostEstimate(
            flops=10 * slots * rows * rows * count * WIDE * 4,
            bytes_accessed=16 * slots * rows * count * WIDE,
            transcendentals=slots * count * 2 * rows * rows,
        ),
        name="attend_back",
    )(jnp.append(lengths, first), fused, totals, up)


def interleave(query, key_rows, value):
    lead = query.shape[0]
    return jnp.stack([one.reshape(lead, -1, WIDE) for one in (query, key_rows, value)], axis=2).reshape(
        lead, -1
    )


def pieces_out(array, count):
    slots, rows, width = array.shape
    return array.reshape(slots, count, rows // count, width).transpose(1, 0, 2, 3)


def spread_out(array):
    count = lax.axis_size("fsdp")
    return lax.all_to_all(pieces_out(array, count), "fsdp", 0, 0, tiled=True)


def bring_in(spread, source):
    count, slots, short, width = spread.shape
    spread = spread.reshape(count * slots, short, width)
    spread = jnp.take(spread, source, axis=0, mode="clip").reshape(count, slots, short, width)
    return lax.all_to_all(spread, "fsdp", 0, 0, tiled=True)


def joined(pieces):
    count, slots, short, width = pieces.shape
    return pieces.transpose(1, 0, 2, 3).reshape(slots, count * short, width)


def per_device(grid, *args):
    (
        tokens,
        cotangent,
        lengths,
        deal,
        w_query,
        b_query,
        w_key,
        w_value,
        b_value,
        w_out,
        b_out,
        gain_one,
        shift_one,
        w_in,
        b_in,
        w_down,
        b_down,
        gain_two,
        shift_two,
    ) = args
    slots, rows, width = tokens.shape
    pairs = width // WIDE
    position = lax.axis_index("fsdp")
    deal_row = deal[0]
    my_lengths = lax.dynamic_slice_in_dim(lengths[0], position * slots, slots)
    spots = jnp.arange(deal_row.shape[0], dtype=jnp.int32)
    inverse = jnp.sum(
        jnp.where(deal_row[None, :] == spots[:, None], spots[None, :], 0), axis=1
    )

    singles = (b_query, b_value, b_out, gain_one, shift_one, b_in, b_down, gain_two, shift_two)
    own, up_own = join(w_query, w_key, w_value, w_out, w_in)
    first = Gather(grid, own)
    got = first.send_line()
    up_whole = lax.all_gather(up_own, BOTH, axis=0, tiled=True)
    small = jnp.concatenate(singles)
    small = jnp.broadcast_to(small[None, :], (grid.total, small.shape[0]))
    cut = pieces_out(cotangent, lax.axis_size("fsdp"))

    got, small, cut, w_down = gate(got, small, cut, w_down)
    first.take_line(got)
    got = first.send_plane()
    down_weights = Gather(grid, w_down)
    got_down = down_weights.send_line()
    small = lax.all_to_all(small, BOTH, 0, 0, tiled=True)

    tokens_own, tokens_other = turn(grid, tokens.reshape(slots * rows, width))
    got, got_down, small, cut, tokens_own, tokens_other = gate(
        got, got_down, small, cut, tokens_own, tokens_other
    )
    first.take_plane(got)
    got = first.send_core()
    down_weights.take_line(got_down)
    got_down = down_weights.send_plane()
    up_spread = lax.all_to_all(cut, "fsdp", 0, 0, tiled=True)
    vectors = []
    at = 0
    for one in singles:
        vectors.append(small[:, at : at + one.shape[0]].reshape(-1).astype(f32))
        at += one.shape[0]
    bq, bv, bo, g1, s1, bi, bd, g2, s2 = vectors
    bias = interleave(bq[None], jnp.zeros_like(bq)[None], bv[None])

    got, bias, tokens = gate(got, bias, tokens)
    qkv = first.whole(got)

    total_rows = slots * rows
    inputs = tokens.reshape(total_rows, width)
    valid = jnp.arange(rows)[None, :] < my_lengths[:, None]
    valid_row = valid.reshape(total_rows)[:, None]

    fused = (matmul(inputs, qkv) + bias).astype(bf16)
    context, totals = attend(fused, my_lengths, slots, 0, slots)
    context_own, context_other = turn(grid, context)
    context, context_own, context_other, up_whole = gate(
        context, context_own, context_other, up_whole
    )
    wo, wi = up_whole[:, :width], up_whole[:, width:]
    tall = w_in.shape[1]

    middle_norm, middle_spread = standardize(inputs.astype(f32) + matmul(context, wo) + bo)
    middle = middle_norm * g1 + s1
    middle_low = middle.astype(bf16)
    middle_low, got_down, up_spread = gate(middle_low, got_down, up_spread)
    down_weights.take_plane(got_down)
    got_down = down_weights.send_core()
    upstream = bring_in(up_spread, deal_row)
    hidden = matmul(middle_low, wi) + bi
    active = gelu_value(hidden).astype(bf16)
    slope = gelu_slope(hidden).astype(bf16)
    active, slope, got_down = gate(active, slope, got_down)
    wd = down_weights.whole(got_down)
    final_norm, final_spread = standardize(middle + matmul(active, wd) + bd)
    output = jnp.where(valid_row, final_norm * g2 + s2, 0.0).astype(bf16)
    output, upstream = gate(output, upstream)

    upstream = joined(upstream).reshape(total_rows, width).astype(f32)
    d_result = jnp.where(valid_row, upstream, 0.0)
    grad_g2 = jnp.sum(d_result * final_norm, axis=0)
    grad_s2 = jnp.sum(d_result, axis=0)
    d_final = norm_back(d_result * g2, final_norm, final_spread)
    d_branch = d_final.astype(bf16)
    grad_bd = jnp.sum(d_branch.astype(f32), axis=0)

    scatter = Scatter(grid)
    out_spread = spread_out(output.reshape(slots, rows, width))
    d_branch, grad_g2, grad_s2, grad_bd = gate(d_branch, grad_g2, grad_s2, grad_bd)
    d_hidden = (right_times(d_branch, wd) * slope.astype(f32)).astype(bf16)
    grad_bi = jnp.sum(d_hidden.astype(f32), axis=0)
    d_hidden, d_branch = gate(d_hidden, d_branch)
    outer = grad_up(middle_low, d_hidden, grad_down(grid, active, d_branch))
    outer, d_hidden, out_spread = gate(outer, d_hidden, out_spread)
    out_pieces = bring_in(out_spread, inverse)
    shard_outer = lax.psum_scatter(outer, BOTH, scatter_dimension=0, tiled=True)
    d_middle = d_final + right_times(d_hidden, wi)
    grad_g1 = jnp.sum(d_middle * middle_norm, axis=0)
    grad_s1 = jnp.sum(d_middle, axis=0)
    d_sum = norm_back(d_middle * g1, middle_norm, middle_spread)
    d_attended = d_sum.astype(bf16)
    grad_bo = jnp.sum(d_attended.astype(f32), axis=0)
    half = pairs // 2
    d_context = right_times(d_attended, wo).astype(bf16)
    d_first, sums_first = attend_back(fused, totals, d_context, my_lengths, slots, 0, half)
    others = [
        matmul(context_other, d_attended).astype(bf16),
        matmul(tokens_other, d_first).astype(bf16),
    ]
    others, d_context, d_attended, d_first, grad_bi = gate(
        others, d_context, d_attended, d_first, grad_bi
    )
    got_first = scatter.send_core(others)
    own_first = [
        matmul(context_own, d_attended).astype(bf16),
        matmul(tokens_own, d_first).astype(bf16),
    ]
    own_first, got_first, d_context, out_pieces = gate(own_first, got_first, d_context, out_pieces)
    got_first = scatter.send_plane(own_first, got_first)
    d_context, got_first[0] = gate(d_context, got_first[0])
    d_second, sums_second = attend_back(
        fused, totals, d_context, my_lengths, slots, half, pairs - half
    )
    other = matmul(tokens_other, d_second).astype(bf16)
    partial = d_sum + right_times(d_first, qkv[:, : half * 3 * WIDE])
    other, d_second, sums_second, partial, got_first = gate(
        other, d_second, sums_second, partial, got_first
    )
    got_second = scatter.send_core([other])
    own_second = matmul(tokens_own, d_second).astype(bf16)
    own_second, d_second, got_second = gate(own_second, d_second, got_second)
    got_second = scatter.send_plane([own_second], got_second)
    got_second[0], d_second, sums_second = gate(got_second[0], d_second, sums_second)
    input_grad = partial + right_times(d_second, qkv[:, half * 3 * WIDE :])
    input_grad = input_grad.astype(bf16).reshape(slots, rows, width)
    sums = jnp.sum(jnp.concatenate([sums_first, sums_second], axis=-1), axis=0)
    input_grad, got_second, got_first = gate(input_grad, got_second, got_first)
    got = scatter.send_line([got_first, got_second])
    shard = scatter.finish(got)
    layer_out = joined(out_pieces)
    shard_qkv = shard[:, width:].reshape(-1, pairs, 3, WIDE)
    shard_down = shard_outer[:, :tall].reshape(shard_outer.shape[0], -1, width).transpose(1, 0, 2)
    shard_q, shard_k, shard_v = (shard_qkv[:, :, i].reshape(-1, width) for i in range(3))

    grads = (sums[0], sums[1], grad_bo, grad_g1, grad_s1, grad_bi, grad_bd, grad_g2, grad_s2)
    small = jnp.concatenate([one.reshape(grid.total, -1) for one in grads], axis=1)
    small = jnp.sum(lax.all_to_all(small, BOTH, 0, 0, tiled=True), axis=0)
    parts = []
    at = 0
    for one in singles:
        parts.append(small[at : at + one.shape[0]])
        at += one.shape[0]
    pbq, pbv, pbo, pg1, ps1, pbi, pbd, pg2, ps2 = parts
    return (
        layer_out,
        input_grad,
        shard_q,
        pbq,
        shard_k,
        shard_v,
        pbv,
        shard[:, :width],
        pbo,
        pg1,
        ps1,
        shard_outer[:, tall:].astype(f32),
        pbi,
        shard_down.astype(f32).reshape(-1, width),
        pbd,
        pg2,
        ps2,
    )


def solution(mesh):
    grid = Grid(mesh)
    rows3 = P(BOTH, None, None)
    rows2 = P(BOTH, None)
    rows1 = P(BOTH)
    table = P("dp", None)
    kinds = (2, 1, 2, 2, 1, 2, 1, 1, 1, 2, 1, 2, 1, 1, 1)
    placed = tuple(rows2 if kind == 2 else rows1 for kind in kinds)

    def step(*args):
        return per_device(grid, *args)

    return jax.shard_map(
        step,
        mesh=mesh,
        in_specs=(rows3, rows3, table, table) + placed,
        out_specs=(rows3, rows3) + placed,
        check_vma=False,
    )
```
